256 devices in a mesh: cube: 8 (over x, core), blk: 32 (over z, y).
Axes of the slice: x: 4, y: 4, z: 8, core: 2. Of those that a mesh axis runs over, the one named last changes fastest.
Arguments:
- right_side: float32 [4, 8, 32, 32, 64], P(None, 'cube', 'blk'), may hold values from -6 to 6
- diag_inverse: float32 [3840, 32768], P('cube', 'blk'), as said below
- panels: float32 [3, 8, 32, 2, 16, 32], P(None, 'cube', 'blk'), may hold values from -1 to 1
- extend_map: int32 [3, 8, 32, 2, 16], P(None, 'cube', 'blk'), may hold values from 0 to 31
Outputs:
- solution: float32 [4, 8, 32, 32, 64], P(None, 'cube', 'blk')
The draws below stay inside these ranges and needn't reach their ends.
Inputs may be any that keep to these rules, and one draw needn't show every extreme that they name: `extend_map`: each entry names one of the 32 parent rows held by the receiving device. `diag_inverse`: dense real entries.
All inputs are finite; a program needn't handle non-finite values.
Results may differ from the reference program's by a relative error of at most 0.0001.
Values sent between devices are 32-bit elements; how exact they have to be, the bound alone decides.
A program may use at most 64 MiB of HBM per device.

```python
import jax
import jax.numpy as jnp
from jax import lax

K = 64
ROWS_DEV = 32
UPD_ROWS = 16
LEVELS = 4
N_CUBE = 8
N_BLK = 32


def draw_diag_inverse(key, part):
    total_rows = N_CUBE * (2 ** LEVELS - 1) * ROWS_DEV
    total_cols = N_BLK * N_BLK * ROWS_DEV
    base = jax.random.normal(key, (total_rows, total_cols), jnp.float32)
    local_block = jnp.arange(total_rows, dtype=jnp.int32) % ((2 ** LEVELS - 1) * ROWS_DEV) // ROWS_DEV
    level_ids = jnp.zeros((total_rows,), jnp.int32)
    for marker in range(1, LEVELS):
        level_ids = level_ids + (local_block >= 2 ** marker - 1).astype(jnp.int32)
    node_rows = N_BLK * ROWS_DEV * jnp.exp2(level_ids.astype(jnp.float32))
    return base * lax_rsqrt(node_rows)[:, None]


def lax_rsqrt(values):
    return 1.0 / jnp.sqrt(values)


def touch_ends(array, rng, smallest, top_value):
    shape = array.shape
    place = [jax.random.randint(jax.random.fold_in(rng, axis), (), 0, shape[axis]) for axis in range(len(shape))]
    array = array.at[tuple(place)].set(smallest)
    longest = shape.index(max(shape))
    place[longest] = (place[longest] + 1) % shape[longest]
    return array.at[tuple(place)].set(top_value)


def block_scale(rng, extent, shards, low, largest):
    loudness = 1.0
    for position, shards_of in shards:
        steps = jax.random.uniform(jax.random.fold_in(jax.random.fold_in(rng, 6), position), (shards_of,), jnp.float32, low / len(shards), largest / len(shards))
        loudness = loudness * jnp.repeat(jnp.exp(steps), extent[position] // shards_of).reshape((-1,) + (1,) * (len(extent) - 1 - position))
    return loudness


def bell_draw(rng, dims, deviation, reach, pieces=(), kind=jnp.bfloat16):
    factor_of = block_scale(rng, dims, pieces, -0.22, 0.18) if pieces else 1.0
    result = jax.random.normal(rng, dims, jnp.float32) * deviation * factor_of
    return jnp.minimum(jnp.maximum(result, -reach), reach).astype(kind)


def setup_inputs(seed: int = 0) -> dict:
    arg_keys = jax.random.split(jax.random.key(seed), 5)
    return {
        "right_side": bell_draw(arg_keys[0], (LEVELS, N_CUBE, N_BLK, ROWS_DEV, K), 1.0, 6.0, ((1, 8), (2, 32)), jnp.float32),
        "diag_inverse": draw_diag_inverse(jax.random.fold_in(arg_keys[4], 71), 0),
        "panels": bell_draw(arg_keys[2], (LEVELS - 1, N_CUBE, N_BLK, 2, UPD_ROWS, ROWS_DEV), ROWS_DEV ** -0.5, 1.0, ((1, 8), (2, 32)), jnp.float32),
        "extend_map": touch_ends(jax.random.randint(arg_keys[3], (LEVELS - 1, N_CUBE, N_BLK, 2, UPD_ROWS), 0, ROWS_DEV), jax.random.fold_in(arg_keys[3], 1), 0, ROWS_DEV - 1).astype(jnp.int32),
    }


def reference(right_side, diag_inverse, panels, extend_map):
    highest = lax.Precision.HIGHEST
    cube_ids = jnp.arange(N_CUBE, dtype=jnp.int32)
    row_ids = jnp.arange(ROWS_DEV, dtype=jnp.int32)
    inverse_table = diag_inverse.reshape(N_CUBE, (2 ** LEVELS - 1) * ROWS_DEV, N_BLK, N_BLK, ROWS_DEV)
    update = jnp.zeros((N_CUBE, N_BLK, ROWS_DEV, K), jnp.float32)
    solved = []
    onehots = []
    diag_levels = []
    for tree_level in range(LEVELS):
        group_width = 2 ** tree_level
        group_count = N_CUBE // group_width
        offset = (group_width - 1) * ROWS_DEV
        diag_level = inverse_table[:, offset:offset + group_width * ROWS_DEV].reshape(
            group_count, group_width, group_width, ROWS_DEV, N_BLK, N_BLK, ROWS_DEV)
        diag_levels.append(diag_level)
        residual_rows = right_side[tree_level] - update
        grouped = residual_rows.reshape(group_count, group_width, N_BLK, ROWS_DEV, K)
        solved_rows = jnp.einsum("gjpsqbr,gpqsk->gjbrk", diag_level, grouped, precision=highest)
        solved_rows = solved_rows.reshape(N_CUBE, N_BLK, ROWS_DEV, K)
        solved.append(solved_rows)
        if tree_level + 1 < LEVELS:
            onehot = (extend_map[tree_level][..., None] == row_ids).astype(jnp.float32)
            onehots.append(onehot)
            upd_rows = jnp.einsum("cbhmr,cbrk->cbhmk", panels[tree_level], solved_rows, precision=highest)
            extended = jnp.einsum("cbhmt,cbhmk->cbhtk", onehot, upd_rows, precision=highest)
            partner = jnp.bitwise_xor(cube_ids, group_width)
            update = extended[:, :, 0] + extended[partner][:, :, 1]
    results = [None] * LEVELS
    parent = None
    for tree_level in reversed(range(LEVELS)):
        group_width = 2 ** tree_level
        group_count = N_CUBE // group_width
        work_rows = solved[tree_level]
        if parent is not None:
            partner = jnp.bitwise_xor(cube_ids, group_width)
            parent_pair = jnp.stack([parent, parent[partner]], axis=2)
            fetched = jnp.einsum("cbhmt,cbhtk->cbhmk", onehots[tree_level], parent_pair, precision=highest)
            work_rows = work_rows - jnp.einsum("cbhmr,cbhmk->cbrk", panels[tree_level], fetched, precision=highest)
        grouped = work_rows.reshape(group_count, group_width, N_BLK, ROWS_DEV, K)
        answer = jnp.einsum("gjpsqbr,gjbrk->gpqsk", diag_levels[tree_level], grouped, precision=highest)
        parent = answer.reshape(N_CUBE, N_BLK, ROWS_DEV, K)
        results[tree_level] = parent
    return jnp.stack(results)
```

```python
import functools

import jax
import jax.numpy as jnp
from jax import lax
from jax.experimental import pallas as pl
from jax.experimental.pallas import tpu as pltpu
from jax.sharding import PartitionSpec as P

F32 = jnp.float32
BF16 = jnp.bfloat16
LEVELS = 4
ROWS = 32
HALF = 16
K = 64
LANES = 2 * K


def split(value):
    high = value.astype(BF16)
    return high, (value - high.astype(F32)).astype(BF16)


def dot(a, b):
    return jnp.dot(a, b, preferred_element_type=F32)


def dot3(a_high, a_low, b):
    b_high, b_low = split(b)
    return dot(a_high, b_high) + (dot(a_high, b_low) + dot(a_low, b_high))


def exact(a, b):
    return jnp.dot(a, b, precision=lax.Precision.HIGHEST, preferred_element_type=F32)


def pack(rows):
    count = rows.shape[0] // ROWS
    parts = rows.reshape(count, 2, HALF, K)
    return jnp.concatenate([parts[:, 0], parts[:, 1]], axis=-1)


def unpack(packed):
    count = packed.shape[0]
    parts = jnp.stack([packed[:, :, :K], packed[:, :, K:]], axis=1)
    return parts.reshape(count * ROWS, K)


def kernel(
    n_cube,
    n_blk,
    rhs_ref,
    diag_ref,
    panels_ref,
    maps_ref,
    out_ref,
    dt_high,
    dt_low,
    d_high,
    d_low,
    mats,
    mats_t,
    solved,
    part,
    rs_recv,
    gather,
    spread,
    sums_send,
    sums_recv,
    rs_send_sem,
    rs_recv_sem,
    ag_send_sem,
    ag_recv_sem,
    up_send_sem,
    up_recv_sem,
    down_send_sem,
    down_recv_sem,
):
    cube = lax.axis_index("cube")
    blk = lax.axis_index("blk")

    def device(c, b):
        return {"cube": c, "blk": b}

    barrier = pltpu.get_barrier_semaphore()

    def greet_blk(step, carry):
        pl.semaphore_signal(
            barrier, inc=1, device_id=device(cube, lax.rem(blk + step, n_blk)),
            device_id_type=pl.DeviceIdType.MESH,
        )
        return carry

    def greet_cube(step, carry):
        pl.semaphore_signal(
            barrier, inc=1, device_id=device(lax.rem(cube + step, n_cube), blk),
            device_id_type=pl.DeviceIdType.MESH,
        )
        return carry

    lax.fori_loop(1, n_blk, greet_blk, 0)
    lax.fori_loop(1, n_cube, greet_cube, 0)

    def rows_of(level):
        return pl.ds((2**level - 1) * ROWS, 2**level * ROWS)

    def prepare_forward(level):
        high, low = split(diag_ref[rows_of(level), :].T)
        dt_high[level, :, : 2**level * ROWS] = high
        dt_low[level, :, : 2**level * ROWS] = low

    def prepare_backward(level):
        high, low = split(diag_ref[rows_of(level), :])
        d_high[rows_of(level), :] = high
        d_low[rows_of(level), :] = low

    def prepare_maps(level):
        row_ids = lax.broadcasted_iota(jnp.int32, (ROWS, HALF), 0)
        for half in range(2):
            onehot = (row_ids == maps_ref[level, half : half + 1, :]).astype(F32)
            mat = exact(onehot, panels_ref[level, half])
            mats[level, half] = mat
            mats_t[level, half] = mat.T

    def wait_for(ref, sem):
        pltpu.make_async_copy(ref, ref, sem).wait()

    def scatter_start(level):
        def step(i, carry):
            to = lax.rem(blk + i, n_blk)
            pltpu.make_async_remote_copy(
                src_ref=part.at[level, to],
                dst_ref=rs_recv.at[level, blk],
                send_sem=rs_send_sem.at[level],
                recv_sem=rs_recv_sem.at[level],
                device_id=device(cube, to),
                device_id_type=pl.DeviceIdType.MESH,
            ).start()
            return carry

        lax.fori_loop(1, n_blk, step, 0)

    def gather_start(level):
        def step(i, carry):
            to = lax.rem(blk + i, n_blk)
            pltpu.make_async_remote_copy(
                src_ref=gather.at[level, blk],
                dst_ref=gather.at[level, blk],
                send_sem=ag_send_sem.at[level],
                recv_sem=ag_recv_sem.at[level],
                device_id=device(cube, to),
                device_id_type=pl.DeviceIdType.MESH,
            ).start()
            return carry

        lax.fori_loop(1, n_blk, step, 0)

    others = pl.ds(0, n_blk - 1)
    prepare_forward(0)
    entry = rhs_ref[0]
    for level in range(LEVELS):
        width = 2**level
        span = width * ROWS
        products = dot3(dt_high[level, :, :span], dt_low[level, :, :span], entry)
        packed = pack(products)
        part[level] = packed
        if level == 0:
            pl.semaphore_wait(barrier, n_blk + n_cube - 2)
        scatter_start(level)
        rs_recv[level, blk] = part[level, blk]
        if level + 1 < LEVELS:
            prepare_maps(level)
            prepare_forward(level + 1)
        else:
            for other in range(LEVELS):
                prepare_backward(other)
        wait_for(rs_recv.at[level, others], rs_recv_sem.at[level])
        solved_packed = jnp.sum(rs_recv[level], axis=0)
        if level + 1 == LEVELS:
            gather[level, blk] = solved_packed
            break
        solved_rows = unpack(solved_packed[None])
        solved[level] = solved_rows
        reach = 2 * width
        base = cube - lax.rem(cube, reach)
        mine = lax.rem(cube, reach)
        kept = rhs_ref[level + 1] - exact(mats[level, 0], solved_rows)
        given = exact(mats[level, 1], solved_rows)
        spread[level, mine, 0] = pack(kept)[0]
        spread[level, mine, 1] = pack(given)[0]

        def up(i, carry, level=level, base=base, mine=mine, reach=reach):
            pltpu.make_async_remote_copy(
                src_ref=spread.at[level, mine],
                dst_ref=spread.at[level, mine],
                send_sem=up_send_sem.at[level],
                recv_sem=up_recv_sem.at[level],
                device_id=device(base + lax.rem(mine + i, reach), blk),
                device_id_type=pl.DeviceIdType.MESH,
            ).start()
            return carry

        lax.fori_loop(1, reach, up, 0)
        wait_for(spread.at[level, pl.ds(0, reach - 1)], up_recv_sem.at[level])
        entry = unpack(
            jnp.stack(
                [
                    spread[level, p, 0] - spread[level, p ^ width, 1]
                    for p in range(reach)
                ]
            )
        )

    for level in reversed(range(LEVELS)):
        width = 2**level
        gather_start(level)
        wait_for(gather.at[level, others], ag_recv_sem.at[level])
        work = unpack(gather[level])
        products = dot3(d_high[rows_of(level), :], d_low[rows_of(level), :], work)
        if level == 0:
            out_ref[0] = products
            break
        packed = pack(products)
        base = cube - lax.rem(cube, width)
        mine = lax.rem(cube, width)
        for p in range(width):
            sums_send[level - 1, p, 0] = packed[p]
            sums_send[level - 1, p, 1] = packed[p ^ (width // 2)]

        def down(i, carry, level=level, base=base, mine=mine, width=width):
            to = lax.rem(mine + i, width)
            pltpu.make_async_remote_copy(
                src_ref=sums_send.at[level - 1, to],
                dst_ref=sums_recv.at[level - 1, mine],
                send_sem=down_send_sem.at[level - 1],
                recv_sem=down_recv_sem.at[level - 1],
                device_id=device(base + to, blk),
                device_id_type=pl.DeviceIdType.MESH,
            ).start()
            return carry

        lax.fori_loop(1, width, down, 0)
        sums_recv[level - 1, mine] = sums_send[level - 1, mine]
        wait_for(
            sums_recv.at[level - 1, pl.ds(0, width - 1)], down_recv_sem.at[level - 1]
        )
        totals = sums_recv[level - 1, 0]
        for p in range(1, width):
            totals = totals + sums_recv[level - 1, p]
        both = unpack(totals)
        own, sibling = both[:ROWS], both[ROWS:]
        out_ref[level] = own
        left = (
            solved[level - 1]
            - exact(mats_t[level - 1, 0], own)
            - exact(mats_t[level - 1, 1], sibling)
        )
        gather[level - 1, blk] = pack(left)[0]

    for level in range(LEVELS):
        wait_for(part.at[level, others], rs_send_sem.at[level])
        wait_for(gather.at[level, others], ag_send_sem.at[level])
        if level + 1 < LEVELS:
            rest = pl.ds(0, 2 * 2**level - 1)
            wait_for(spread.at[level, rest], up_send_sem.at[level])
            wait_for(sums_send.at[level, rest], down_send_sem.at[level])


def body(n_cube, n_blk, right_side, diag_inverse, panels, extend_map):
    rhs = right_side[:, 0, 0]
    blocks = panels[:, 0, 0]
    maps = extend_map[:, 0, 0]
    rows, columns = diag_inverse.shape
    widest = 2 ** (LEVELS - 1)
    vmem = pl.BlockSpec(memory_space=pltpu.VMEM)
    chunks = pltpu.VMEM((LEVELS, n_blk, HALF, LANES), F32)
    pairs = pltpu.VMEM((LEVELS - 1, widest, 2, HALF, LANES), F32)
    result = pl.pallas_call(
        functools.partial(kernel, n_cube, n_blk),
        out_shape=jax.ShapeDtypeStruct(rhs.shape, F32),
        in_specs=[vmem] * 4,
        out_specs=vmem,
        scratch_shapes=[
            pltpu.VMEM((LEVELS, columns, widest * ROWS), BF16),
            pltpu.VMEM((LEVELS, columns, widest * ROWS), BF16),
            pltpu.VMEM((rows, columns), BF16),
            pltpu.VMEM((rows, columns), BF16),
            pltpu.VMEM((LEVELS - 1, 2, ROWS, ROWS), F32),
            pltpu.VMEM((LEVELS - 1, 2, ROWS, ROWS), F32),
            pltpu.VMEM((LEVELS - 1, ROWS, K), F32),
            chunks,
            chunks,
            chunks,
            pairs,
            pairs,
            pairs,
        ]
        + [pltpu.SemaphoreType.DMA((LEVELS,))] * 4
        + [pltpu.SemaphoreType.DMA((LEVELS - 1,))] * 4,
        compiler_params=pltpu.CompilerParams(
            collective_id=0, has_side_effects=True, vmem_limit_bytes=48 * 2**20
        ),
    )(rhs, diag_inverse, blocks, maps)
    return result[:, None, None]


def solution(mesh):
    placed = (
        P(None, "cube", "blk", None, None),
        P("cube", "blk"),
        P(None, "cube", "blk", None, None, None),
        P(None, "cube", "blk", None, None),
    )
    return jax.shard_map(
        functools.partial(body, mesh.shape["cube"], mesh.shape["blk"]),
        mesh=mesh,
        in_specs=placed,
        out_specs=P(None, "cube", "blk", None, None),
        check_vma=False,
    )
```

```python
import functools

import jax
import jax.numpy as jnp
from jax import lax
from jax.experimental import pallas as pl
from jax.experimental.pallas import tpu as pltpu
from jax.sharding import PartitionSpec as P

F32 = jnp.float32
BF16 = jnp.bfloat16
LEVELS = 4
ROWS = 32
HALF = 16
K = 64
LANES = 2 * K
N_Y = 4


def split(value):
    high = value.astype(BF16)
    return high, (value - high.astype(F32)).astype(BF16)


def dot(a, b):
    return jnp.dot(a, b, preferred_element_type=F32)


def dot3(a_high, a_low, b):
    b_high, b_low = split(b)
    return dot(a_high, b_high) + (dot(a_high, b_low) + dot(a_low, b_high))


def exact(a, b):
    return jnp.dot(a, b, precision=lax.Precision.HIGHEST, preferred_element_type=F32)


def pack(rows):
    count = rows.shape[0] // ROWS
    parts = rows.reshape(count, 2, HALF, K)
    return jnp.concatenate([parts[:, 0], parts[:, 1]], axis=-1)


def unpack(packed):
    count = packed.shape[0]
    parts = jnp.stack([packed[:, :, :K], packed[:, :, K:]], axis=1)
    return parts.reshape(count * ROWS, K)


def kernel(
    n_cube,
    n_blk,
    rhs_hbm,
    diag_hbm,
    panels_hbm,
    maps_hbm,
    out_ref,
    rhs_ref,
    diag_ref,
    panels_ref,
    maps_ref,
    dt_high,
    dt_low,
    d_high,
    d_low,
    mats,
    mats_t,
    solved,
    part,
    rs_recv,
    gather,
    spread,
    sums_send,
    sums_recv,
    rs_send_sem,
    rs_recv_sem,
    ag_send_sem,
    ag_recv_sem,
    up_send_sem,
    up_recv_sem,
    down_send_sem,
    down_recv_sem,
    load_sem,
):
    cube = lax.axis_index("cube")
    blk = lax.axis_index("blk")

    n_y = min(N_Y, n_blk)
    depth = n_blk // n_y
    plane = blk // n_y
    column = lax.rem(blk, n_y)
    ring = sorted(
        [(dz, dy) for dz in range(depth) for dy in range(n_y) if dz + dy],
        key=lambda at: -(min(at[0], depth - at[0]) + min(at[1], n_y - at[1])),
    )

    def peer(place):
        return lax.rem(plane + place[0], depth) * n_y + lax.rem(column + place[1], n_y)

    def device(c, b):
        return {"cube": c, "blk": b}

    def rows_of(level):
        return pl.ds((2**level - 1) * ROWS, 2**level * ROWS)

    diag_loads = [
        pltpu.make_async_copy(
            diag_hbm.at[rows_of(level), :],
            diag_ref.at[rows_of(level), :],
            load_sem.at[level],
        )
        for level in range(LEVELS)
    ]
    rhs_load = pltpu.make_async_copy(rhs_hbm, rhs_ref, load_sem.at[LEVELS])
    panels_load = pltpu.make_async_copy(panels_hbm, panels_ref, load_sem.at[LEVELS + 1])
    maps_load = pltpu.make_async_copy(maps_hbm, maps_ref, load_sem.at[LEVELS + 2])
    diag_loads[0].start()
    rhs_load.start()
    panels_load.start()
    maps_load.start()
    for load in diag_loads[1:]:
        load.start()

    barrier = pltpu.get_barrier_semaphore()

    def greet_blk(step, carry):
        pl.semaphore_signal(
            barrier, inc=1, device_id=device(cube, lax.rem(blk + step, n_blk)),
            device_id_type=pl.DeviceIdType.MESH,
        )
        return carry

    def greet_cube(step, carry):
        pl.semaphore_signal(
            barrier, inc=1, device_id=device(lax.rem(cube + step, n_cube), blk),
            device_id_type=pl.DeviceIdType.MESH,
        )
        return carry

    lax.fori_loop(1, n_blk, greet_blk, 0)
    lax.fori_loop(1, n_cube, greet_cube, 0)

    def prepare_forward(level):
        diag_loads[level].wait()
        high, low = split(diag_ref[rows_of(level), :].T)
        dt_high[level, :, : 2**level * ROWS] = high
        dt_low[level, :, : 2**level * ROWS] = low

    def prepare_backward(level):
        high, low = split(diag_ref[rows_of(level), :])
        d_high[rows_of(level), :] = high
        d_low[rows_of(level), :] = low

    def prepare_maps(level):
        row_ids = lax.broadcasted_iota(jnp.int32, (ROWS, HALF), 0)
        for half in range(2):
            onehot = (row_ids == maps_ref[level, half : half + 1, :]).astype(F32)
            mat = exact(onehot, panels_ref[level, half])
            mats[level, half] = mat
            mats_t[level, half] = mat.T

    def wait_for(ref, sem):
        pltpu.make_async_copy(ref, ref, sem).wait()

    def scatter_start(level):
        def step(place):
            to = peer(place)
            pltpu.make_async_remote_copy(
                src_ref=part.at[level, to],
                dst_ref=rs_recv.at[level, blk],
                send_sem=rs_send_sem.at[level],
                recv_sem=rs_recv_sem.at[level],
                device_id=device(cube, to),
                device_id_type=pl.DeviceIdType.MESH,
            ).start()

        for place in ring:
            step(place)

    def gather_start(level):
        def step(place):
            to = peer(place)
            pltpu.make_async_remote_copy(
                src_ref=gather.at[level, blk],
                dst_ref=gather.at[level, blk],
                send_sem=ag_send_sem.at[level],
                recv_sem=ag_recv_sem.at[level],
                device_id=device(cube, to),
                device_id_type=pl.DeviceIdType.MESH,
            ).start()

        for place in ring:
            step(place)

    others = pl.ds(0, n_blk - 1)
    prepare_forward(0)
    rhs_load.wait()
    entry = rhs_ref[0]
    for level in range(LEVELS):
        width = 2**level
        span = width * ROWS
        products = dot3(dt_high[level, :, :span], dt_low[level, :, :span], entry)
        packed = pack(products)
        part[level] = packed
        if level == 0:
            pl.semaphore_wait(barrier, n_blk + n_cube - 2)
        scatter_start(level)
        rs_recv[level, blk] = part[level, blk]
        if level == 0:
            panels_load.wait()
            maps_load.wait()
        if level + 1 < LEVELS:
            prepare_maps(level)
            prepare_forward(level + 1)
        else:
            for other in range(LEVELS):
                prepare_backward(other)
        wait_for(rs_recv.at[level, others], rs_recv_sem.at[level])
        solved_packed = jnp.sum(rs_recv[level], axis=0)
        if level + 1 == LEVELS:
            gather[level, blk] = solved_packed
            break
        solved_rows = unpack(solved_packed[None])
        solved[level] = solved_rows
        reach = 2 * width
        base = cube - lax.rem(cube, reach)
        mine = lax.rem(cube, reach)
        kept = rhs_ref[level + 1] - exact(mats[level, 0], solved_rows)
        given = exact(mats[level, 1], solved_rows)
        spread[level, mine, 0] = pack(kept)[0]
        spread[level, mine, 1] = pack(given)[0]

        def up(i, carry, level=level, base=base, mine=mine, reach=reach):
            pltpu.make_async_remote_copy(
                src_ref=spread.at[level, mine],
                dst_ref=spread.at[level, mine],
                send_sem=up_send_sem.at[level],
                recv_sem=up_recv_sem.at[level],
                device_id=device(base + lax.rem(mine + i, reach), blk),
                device_id_type=pl.DeviceIdType.MESH,
            ).start()
            return carry

        lax.fori_loop(1, reach, up, 0)
        wait_for(spread.at[level, pl.ds(0, reach - 1)], up_recv_sem.at[level])
        entry = unpack(
            jnp.stack(
                [
                    spread[level, p, 0] - spread[level, p ^ width, 1]
                    for p in range(reach)
                ]
            )
        )

    for level in reversed(range(LEVELS)):
        width = 2**level
        gather_start(level)
        wait_for(gather.at[level, others], ag_recv_sem.at[level])
        work = unpack(gather[level])
        products = dot3(d_high[rows_of(level), :], d_low[rows_of(level), :], work)
        if level == 0:
            out_ref[0] = products
            break
        packed = pack(products)
        base = cube - lax.rem(cube, width)
        mine = lax.rem(cube, width)
        for p in range(width):
            sums_send[level - 1, p, 0] = packed[p]
            sums_send[level - 1, p, 1] = packed[p ^ (width // 2)]

        def down(i, carry, level=level, base=base, mine=mine, width=width):
            to = lax.rem(mine + i, width)
            pltpu.make_async_remote_copy(
                src_ref=sums_send.at[level - 1, to],
                dst_ref=sums_recv.at[level - 1, mine],
                send_sem=down_send_sem.at[level - 1],
                recv_sem=down_recv_sem.at[level - 1],
                device_id=device(base + to, blk),
                device_id_type=pl.DeviceIdType.MESH,
            ).start()
            return carry

        lax.fori_loop(1, width, down, 0)
        sums_recv[level - 1, mine] = sums_send[level - 1, mine]
        wait_for(
            sums_recv.at[level - 1, pl.ds(0, width - 1)], down_recv_sem.at[level - 1]
        )
        totals = sums_recv[level - 1, 0]
        for p in range(1, width):
            totals = totals + sums_recv[level - 1, p]
        both = unpack(totals)
        own, sibling = both[:ROWS], both[ROWS:]
        out_ref[level] = own
        left = (
            solved[level - 1]
            - exact(mats_t[level - 1, 0], own)
            - exact(mats_t[level - 1, 1], sibling)
        )
        gather[level - 1, blk] = pack(left)[0]

    for level in range(LEVELS):
        wait_for(part.at[level, others], rs_send_sem.at[level])
        wait_for(gather.at[level, others], ag_send_sem.at[level])
        if level + 1 < LEVELS:
            rest = pl.ds(0, 2 * 2**level - 1)
            wait_for(spread.at[level, rest], up_send_sem.at[level])
            wait_for(sums_send.at[level, rest], down_send_sem.at[level])


def body(n_cube, n_blk, right_side, diag_inverse, panels, extend_map):
    rhs = right_side[:, 0, 0]
    blocks = panels[:, 0, 0]
    maps = extend_map[:, 0, 0]
    rows, columns = diag_inverse.shape
    widest = 2 ** (LEVELS - 1)
    vmem = pl.BlockSpec(memory_space=pltpu.VMEM)
    chunks = pltpu.VMEM((LEVELS, n_blk, HALF, LANES), F32)
    pairs = pltpu.VMEM((LEVELS - 1, widest, 2, HALF, LANES), F32)
    result = pl.pallas_call(
        functools.partial(kernel, n_cube, n_blk),
        out_shape=jax.ShapeDtypeStruct(rhs.shape, F32),
        in_specs=[pl.BlockSpec(memory_space=pltpu.HBM)] * 4,
        out_specs=vmem,
        scratch_shapes=[
            pltpu.VMEM(rhs.shape, F32),
            pltpu.VMEM(diag_inverse.shape, F32),
            pltpu.VMEM(blocks.shape, F32),
            pltpu.VMEM(maps.shape, jnp.int32),
            pltpu.VMEM((LEVELS, columns, widest * ROWS), BF16),
            pltpu.VMEM((LEVELS, columns, widest * ROWS), BF16),
            pltpu.VMEM((rows, columns), BF16),
            pltpu.VMEM((rows, columns), BF16),
            pltpu.VMEM((LEVELS - 1, 2, ROWS, ROWS), F32),
            pltpu.VMEM((LEVELS - 1, 2, ROWS, ROWS), F32),
            pltpu.VMEM((LEVELS - 1, ROWS, K), F32),
            chunks,
            chunks,
            chunks,
            pairs,
            pairs,
            pairs,
        ]
        + [pltpu.SemaphoreType.DMA((LEVELS,))] * 4
        + [pltpu.SemaphoreType.DMA((LEVELS - 1,))] * 4
        + [pltpu.SemaphoreType.DMA((LEVELS + 3,))],
        compiler_params=pltpu.CompilerParams(
            collective_id=0, has_side_effects=True, vmem_limit_bytes=62 * 2**20
        ),
    )(rhs, diag_inverse, blocks, maps)
    return result[:, None, None]


def solution(mesh):
    placed = (
        P(None, "cube", "blk", None, None),
        P("cube", "blk"),
        P(None, "cube", "blk", None, None, None),
        P(None, "cube", "blk", None, None),
    )
    return jax.shard_map(
        functools.partial(body, mesh.shape["cube"], mesh.shape["blk"]),
        mesh=mesh,
        in_specs=placed,
        out_specs=P(None, "cube", "blk", None, None),
        check_vma=False,
    )
```

```python
import functools

import jax
import jax.numpy as jnp
from jax import lax
from jax.experimental import pallas as pl
from jax.experimental.pallas import tpu as pltpu
from jax.sharding import PartitionSpec as P

F32 = jnp.float32
BF16 = jnp.bfloat16
LEVELS = 4
ROWS = 32
MAPPED = 16
K = 64
STREAMS = 2
COLS = K // STREAMS
LANES = 128
FOLD = LANES // COLS
SUB = ROWS // FOLD
N_Y = 4


def split(value):
    high = value.astype(BF16)
    return high, (value - high.astype(F32)).astype(BF16)


def dot(a, b):
    return jnp.dot(a, b, preferred_element_type=F32)


def dot3(a_high, a_low, b):
    b_high, b_low = split(b)
    wide = dot(a_high, jnp.concatenate([b_high, b_low], axis=1))
    return wide[:, :COLS] + (wide[:, COLS:] + dot(a_low, b_high))


def exact(a, b):
    return jnp.dot(a, b, precision=lax.Precision.HIGHEST, preferred_element_type=F32)


def pack(rows):
    count = rows.shape[0] // ROWS
    parts = rows.reshape(count, FOLD, SUB, COLS)
    return jnp.concatenate([parts[:, i] for i in range(FOLD)], axis=-1)


def unpack(packed):
    count = packed.shape[0]
    parts = [packed[:, :, i * COLS : (i + 1) * COLS] for i in range(FOLD)]
    return jnp.stack(parts, axis=1).reshape(count * ROWS, COLS)


def kernel(
    n_cube,
    n_blk,
    rhs_hbm,
    diag_hbm,
    panels_hbm,
    maps_hbm,
    out_ref,
    rhs_ref,
    diag_ref,
    panels_ref,
    maps_ref,
    dt_high,
    dt_low,
    d_high,
    d_low,
    mats,
    mats_t,
    solved,
    part,
    rs_recv,
    gather,
    spread,
    sums_send,
    sums_recv,
    rs_send_sem,
    rs_recv_sem,
    ag_send_sem,
    ag_recv_sem,
    up_send_sem,
    up_recv_sem,
    down_send_sem,
    down_recv_sem,
    load_sem,
):
    cube = lax.axis_index("cube")
    blk = lax.axis_index("blk")

    n_y = min(N_Y, n_blk)
    depth = n_blk // n_y
    plane = blk // n_y
    column = lax.rem(blk, n_y)
    ring = sorted(
        [(dz, dy) for dz in range(depth) for dy in range(n_y) if dz + dy],
        key=lambda at: -(min(at[0], depth - at[0]) + min(at[1], n_y - at[1])),
    )

    def peer(place):
        return lax.rem(plane + place[0], depth) * n_y + lax.rem(column + place[1], n_y)

    def device(c, b):
        return {"cube": c, "blk": b}

    def rows_of(level):
        return pl.ds((2**level - 1) * ROWS, 2**level * ROWS)

    diag_loads = [
        pltpu.make_async_copy(
            diag_hbm.at[rows_of(level), :],
            diag_ref.at[rows_of(level), :],
            load_sem.at[level],
        )
        for level in range(LEVELS)
    ]
    rhs_load = pltpu.make_async_copy(rhs_hbm, rhs_ref, load_sem.at[LEVELS])
    panels_load = pltpu.make_async_copy(panels_hbm, panels_ref, load_sem.at[LEVELS + 1])
    maps_load = pltpu.make_async_copy(maps_hbm, maps_ref, load_sem.at[LEVELS + 2])
    diag_loads[0].start()
    rhs_load.start()
    panels_load.start()
    maps_load.start()
    for load in diag_loads[1:]:
        load.start()

    barrier = pltpu.get_barrier_semaphore()

    def greet_blk(step, carry):
        pl.semaphore_signal(
            barrier, inc=1, device_id=device(cube, lax.rem(blk + step, n_blk)),
            device_id_type=pl.DeviceIdType.MESH,
        )
        return carry

    def greet_cube(step, carry):
        pl.semaphore_signal(
            barrier, inc=1, device_id=device(lax.rem(cube + step, n_cube), blk),
            device_id_type=pl.DeviceIdType.MESH,
        )
        return carry

    lax.fori_loop(1, n_blk, greet_blk, 0)
    lax.fori_loop(1, n_cube, greet_cube, 0)

    def prepare_forward(level):
        diag_loads[level].wait()
        high, low = split(diag_ref[rows_of(level), :].T)
        dt_high[level, :, : 2**level * ROWS] = high
        dt_low[level, :, : 2**level * ROWS] = low

    def prepare_backward(level):
        high, low = split(diag_ref[rows_of(level), :])
        d_high[rows_of(level), :] = high
        d_low[rows_of(level), :] = low

    def prepare_maps(level):
        row_ids = lax.broadcasted_iota(jnp.int32, (ROWS, MAPPED), 0)
        for half in range(2):
            onehot = (row_ids == maps_ref[level, half : half + 1, :]).astype(F32)
            mat = exact(onehot, panels_ref[level, half])
            mats[level, half] = mat
            mats_t[level, half] = mat.T

    def wait_for(ref, sem):
        pltpu.make_async_copy(ref, ref, sem).wait()

    def scatter_start(stream, level):
        def step(place):
            to = peer(place)
            pltpu.make_async_remote_copy(
                src_ref=part.at[stream, level, to],
                dst_ref=rs_recv.at[stream, level, blk],
                send_sem=rs_send_sem.at[stream, level],
                recv_sem=rs_recv_sem.at[stream, level],
                device_id=device(cube, to),
                device_id_type=pl.DeviceIdType.MESH,
            ).start()

        for place in ring:
            step(place)

    def gather_start(stream, level):
        def step(place):
            to = peer(place)
            pltpu.make_async_remote_copy(
                src_ref=gather.at[stream, level, blk],
                dst_ref=gather.at[stream, level, blk],
                send_sem=ag_send_sem.at[stream, level],
                recv_sem=ag_recv_sem.at[stream, level],
                device_id=device(cube, to),
                device_id_type=pl.DeviceIdType.MESH,
            ).start()

        for place in ring:
            step(place)

    others = pl.ds(0, n_blk - 1)
    streams = range(STREAMS)

    def columns_of(stream):
        return pl.ds(stream * COLS, COLS)

    def scatter(stream, level, entry):
        span = 2**level * ROWS
        products = dot3(dt_high[level, :, :span], dt_low[level, :, :span], entry)
        part[stream, level] = pack(products)
        if level == 0 and stream == 0:
            pl.semaphore_wait(barrier, n_blk + n_cube - 2)
        scatter_start(stream, level)
        rs_recv[stream, level, blk] = part[stream, level, blk]

    def climb(stream, level):
        wait_for(rs_recv.at[stream, level, others], rs_recv_sem.at[stream, level])
        solved_packed = jnp.sum(rs_recv[stream, level], axis=0)
        if level + 1 == LEVELS:
            gather[stream, level, blk] = solved_packed
            gather_start(stream, level)
            return
        solved_rows = unpack(solved_packed[None])
        solved[stream, level] = solved_rows
        width = 2**level
        reach = 2 * width
        base = cube - lax.rem(cube, reach)
        mine = lax.rem(cube, reach)
        kept = rhs_ref[level + 1, :, columns_of(stream)] - exact(mats[level, 0], solved_rows)
        given = exact(mats[level, 1], solved_rows)
        spread[stream, level, mine, 0] = pack(kept)[0]
        spread[stream, level, mine, 1] = pack(given)[0]

        def up(i, carry):
            pltpu.make_async_remote_copy(
                src_ref=spread.at[stream, level, mine],
                dst_ref=spread.at[stream, level, mine],
                send_sem=up_send_sem.at[stream, level],
                recv_sem=up_recv_sem.at[stream, level],
                device_id=device(base + lax.rem(mine + i, reach), blk),
                device_id_type=pl.DeviceIdType.MESH,
            ).start()
            return carry

        lax.fori_loop(1, reach, up, 0)
        wait_for(
            spread.at[stream, level, pl.ds(0, reach - 1)], up_recv_sem.at[stream, level]
        )
        entry = [
            spread[stream, level, p, 0] - spread[stream, level, p ^ width, 1]
            for p in range(reach)
        ]
        scatter(stream, level + 1, unpack(jnp.stack(entry)))

    def descend(stream, level):
        wait_for(gather.at[stream, level, others], ag_recv_sem.at[stream, level])
        work = unpack(gather[stream, level])
        products = dot3(d_high[rows_of(level), :], d_low[rows_of(level), :], work)
        if level == 0:
            out_ref[0, :, columns_of(stream)] = products
            return
        packed = pack(products)
        width = 2**level
        base = cube - lax.rem(cube, width)
        mine = lax.rem(cube, width)
        under = level - 1
        for p in range(width):
            sums_send[stream, under, p, 0] = packed[p]
            sums_send[stream, under, p, 1] = packed[p ^ (width // 2)]

        def down(i, carry):
            to = lax.rem(mine + i, width)
            pltpu.make_async_remote_copy(
                src_ref=sums_send.at[stream, under, to],
                dst_ref=sums_recv.at[stream, under, mine],
                send_sem=down_send_sem.at[stream, under],
                recv_sem=down_recv_sem.at[stream, under],
                device_id=device(base + to, blk),
                device_id_type=pl.DeviceIdType.MESH,
            ).start()
            return carry

        lax.fori_loop(1, width, down, 0)
        sums_recv[stream, under, mine] = sums_send[stream, under, mine]
        wait_for(
            sums_recv.at[stream, under, pl.ds(0, width - 1)],
            down_recv_sem.at[stream, under],
        )
        totals = sums_recv[stream, under, 0]
        for p in range(1, width):
            totals = totals + sums_recv[stream, under, p]
        both = unpack(totals)
        own, sibling = both[:ROWS], both[ROWS:]
        left = (
            solved[stream, under]
            - exact(mats_t[under, 0], own)
            - exact(mats_t[under, 1], sibling)
        )
        gather[stream, under, blk] = pack(left)[0]
        gather_start(stream, under)
        out_ref[level, :, columns_of(stream)] = own

    prepare_forward(0)
    rhs_load.wait()
    for stream in streams:
        scatter(stream, 0, rhs_ref[0, :, columns_of(stream)])
    panels_load.wait()
    maps_load.wait()
    for level in range(LEVELS - 1):
        prepare_maps(level)
        prepare_forward(level + 1)
    for level in range(LEVELS):
        prepare_backward(level)
    for level in range(LEVELS):
        for stream in streams:
            climb(stream, level)
    for level in reversed(range(LEVELS)):
        for stream in streams:
            descend(stream, level)

    for stream in streams:
        for level in range(LEVELS):
            wait_for(part.at[stream, level, others], rs_send_sem.at[stream, level])
            wait_for(gather.at[stream, level, others], ag_send_sem.at[stream, level])
            if level + 1 < LEVELS:
                rest = pl.ds(0, 2 * 2**level - 1)
                wait_for(spread.at[stream, level, rest], up_send_sem.at[stream, level])
                wait_for(
                    sums_send.at[stream, level, rest], down_send_sem.at[stream, level]
                )


def body(n_cube, n_blk, right_side, diag_inverse, panels, extend_map):
    rhs = right_side[:, 0, 0]
    blocks = panels[:, 0, 0]
    maps = extend_map[:, 0, 0]
    rows, columns = diag_inverse.shape
    widest = 2 ** (LEVELS - 1)
    vmem = pl.BlockSpec(memory_space=pltpu.VMEM)
    chunks = pltpu.VMEM((STREAMS, LEVELS, n_blk, SUB, LANES), F32)
    pairs = pltpu.VMEM((STREAMS, LEVELS - 1, widest, 2, SUB, LANES), F32)
    result = pl.pallas_call(
        functools.partial(kernel, n_cube, n_blk),
        out_shape=jax.ShapeDtypeStruct(rhs.shape, F32),
        in_specs=[pl.BlockSpec(memory_space=pltpu.HBM)] * 4,
        out_specs=vmem,
        scratch_shapes=[
            pltpu.VMEM(rhs.shape, F32),
            pltpu.VMEM(diag_inverse.shape, F32),
            pltpu.VMEM(blocks.shape, F32),
            pltpu.VMEM(maps.shape, jnp.int32),
            pltpu.VMEM((LEVELS, columns, widest * ROWS), BF16),
            pltpu.VMEM((LEVELS, columns, widest * ROWS), BF16),
            pltpu.VMEM((rows, columns), BF16),
            pltpu.VMEM((rows, columns), BF16),
            pltpu.VMEM((LEVELS - 1, 2, ROWS, ROWS), F32),
            pltpu.VMEM((LEVELS - 1, 2, ROWS, ROWS), F32),
            pltpu.VMEM((STREAMS, LEVELS - 1, ROWS, COLS), F32),
            chunks,
            chunks,
            chunks,
            pairs,
            pairs,
            pairs,
        ]
        + [pltpu.SemaphoreType.DMA((STREAMS, LEVELS))] * 4
        + [pltpu.SemaphoreType.DMA((STREAMS, LEVELS - 1))] * 4
        + [pltpu.SemaphoreType.DMA((LEVELS + 3,))],
        compiler_params=pltpu.CompilerParams(
            collective_id=0, has_side_effects=True, vmem_limit_bytes=62 * 2**20
        ),
    )(rhs, diag_inverse, blocks, maps)
    return result[:, None, None]


def solution(mesh):
    placed = (
        P(None, "cube", "blk", None, None),
        P("cube", "blk"),
        P(None, "cube", "blk", None, None, None),
        P(None, "cube", "blk", None, None),
    )
    return jax.shard_map(
        functools.partial(body, mesh.shape["cube"], mesh.shape["blk"]),
        mesh=mesh,
        in_specs=placed,
        out_specs=P(None, "cube", "blk", None, None),
        check_vma=False,
    )
```

```python
import functools

import jax
import jax.numpy as jnp
from jax import lax
from jax.experimental import pallas as pl
from jax.experimental.pallas import tpu as pltpu
from jax.sharding import PartitionSpec as P

F32 = jnp.float32
BF16 = jnp.bfloat16
LEVELS = 4
ROWS = 32
MAPPED = 16
K = 64
STREAMS = 2
COLS = K // STREAMS
LANES = 128
FOLD = LANES // COLS
SUB = ROWS // FOLD
N_Y = 4
UP_TURNS = (False, True, True, False)
DOWN_TURNS = (False, False, True, True)


def split(value):
    high = value.astype(BF16)
    return high, (value - high.astype(F32)).astype(BF16)


def dot(a, b):
    return jnp.dot(a, b, preferred_element_type=F32)


def left_terms(value):
    high, low = split(value)
    return jnp.concatenate([high, high, low], axis=1)


def right_terms(value):
    high, low = split(value)
    return jnp.concatenate([high, low, high], axis=0)


def lane_group(shape):
    return lax.broadcasted_iota(jnp.int32, shape, len(shape) - 1) // COLS


def spread_terms(packed):
    count = packed.shape[0]
    high = packed.astype(BF16).astype(F32)
    blocks = []
    for value in (high, packed - high):
        turned = [value] + [pltpu.roll(value, COLS * i, 2) for i in range(1, FOLD)]
        block = []
        for lanes in range(FOLD):
            rows = [turned[(lanes - fold) % FOLD] for fold in range(FOLD)]
            rows = jnp.stack(rows, axis=1)
            rows = jnp.where(lane_group(rows.shape) == lanes, rows, 0.0)
            block.append(rows.reshape(count * ROWS, LANES))
        blocks.append(jnp.concatenate(block, axis=0).astype(BF16))
    return jnp.concatenate([blocks[0], blocks[1], blocks[0]], axis=0)


def collect_terms(terms, count):
    parts = terms.reshape(FOLD, count, FOLD, SUB, LANES)
    group = lane_group((count, SUB, LANES))
    total = None
    for turn in range(FOLD):
        piece = parts[0, :, turn]
        for fold in range(1, FOLD):
            piece = jnp.where(group == fold, parts[fold, :, (fold + turn) % FOLD], piece)
        if turn:
            total = total + pltpu.roll(piece, COLS * turn, 2)
        else:
            total = piece
    return total


def exact(a, b):
    return jnp.dot(a, b, precision=lax.Precision.HIGHEST, preferred_element_type=F32)


def pack(rows):
    count = rows.shape[0] // ROWS
    parts = rows.reshape(count, FOLD, SUB, COLS)
    return jnp.concatenate([parts[:, i] for i in range(FOLD)], axis=-1)


def unpack(packed):
    count = packed.shape[0]
    parts = [packed[:, :, i * COLS : (i + 1) * COLS] for i in range(FOLD)]
    return jnp.stack(parts, axis=1).reshape(count * ROWS, COLS)


def kernel(
    n_cube,
    n_blk,
    rhs_hbm,
    diag_hbm,
    panels_hbm,
    maps_hbm,
    out_ref,
    rhs_ref,
    diag_ref,
    panels_ref,
    maps_ref,
    forward,
    backward,
    mats,
    mats_t,
    solved,
    part,
    rs_recv,
    gather,
    spread,
    sums_send,
    sums_recv,
    rs_send_sem,
    rs_recv_sem,
    ag_send_sem,
    ag_recv_sem,
    up_send_sem,
    up_recv_sem,
    down_send_sem,
    down_recv_sem,
    load_sem,
):
    cube = lax.axis_index("cube")
    blk = lax.axis_index("blk")

    n_y = min(N_Y, n_blk)
    depth = n_blk // n_y
    plane = blk // n_y
    column = lax.rem(blk, n_y)
    ring = sorted(
        [(dz, dy) for dz in range(depth) for dy in range(n_y) if dz + dy],
        key=lambda at: -(min(at[0], depth - at[0]) + min(at[1], n_y - at[1])),
    )

    def peer(place):
        return lax.rem(plane + place[0], depth) * n_y + lax.rem(column + place[1], n_y)

    def members(mine, size):
        chips = size // 2
        order = sorted(
            [(dx, core) for dx in range(chips) for core in range(2) if dx + core],
            key=lambda at: -min(at[0], chips - at[0]),
        )
        return [
            lax.rem(mine // 2 + dx, chips) * 2 + lax.rem(lax.rem(mine, 2) + core, 2)
            for dx, core in order
        ]

    def device(c, b):
        return {"cube": c, "blk": b}

    def rows_of(level):
        return pl.ds((2**level - 1) * ROWS, 2**level * ROWS)

    diag_loads = [
        pltpu.make_async_copy(
            diag_hbm.at[rows_of(level), :],
            diag_ref.at[rows_of(level), :],
            load_sem.at[level],
        )
        for level in range(LEVELS)
    ]
    rhs_load = pltpu.make_async_copy(rhs_hbm, rhs_ref, load_sem.at[LEVELS])
    panels_load = pltpu.make_async_copy(panels_hbm, panels_ref, load_sem.at[LEVELS + 1])
    maps_load = pltpu.make_async_copy(maps_hbm, maps_ref, load_sem.at[LEVELS + 2])
    diag_loads[0].start()
    rhs_load.start()
    panels_load.start()
    maps_load.start()
    for load in diag_loads[1:]:
        load.start()

    barrier = pltpu.get_barrier_semaphore()

    def greet_blk(step, carry):
        pl.semaphore_signal(
            barrier, inc=1, device_id=device(cube, lax.rem(blk + step, n_blk)),
            device_id_type=pl.DeviceIdType.MESH,
        )
        return carry

    def greet_cube(step, carry):
        pl.semaphore_signal(
            barrier, inc=1, device_id=device(lax.rem(cube + step, n_cube), blk),
            device_id_type=pl.DeviceIdType.MESH,
        )
        return carry

    lax.fori_loop(1, n_blk, greet_blk, 0)
    lax.fori_loop(1, n_cube, greet_cube, 0)

    def wide_of(level):
        return slice(3 * FOLD * (2**level - 1) * ROWS, 3 * FOLD * (2**(level + 1) - 1) * ROWS)

    def tall_of(level):
        return slice(FOLD * (2**level - 1) * ROWS, FOLD * (2**(level + 1) - 1) * ROWS)

    def folds_of(level):
        columns = diag_ref[rows_of(level), :].T
        span = columns.shape[1]
        parts = columns.reshape(n_blk, FOLD, SUB, span)
        return [parts[:, i].reshape(n_blk * SUB, span) for i in range(FOLD)]

    def prepare_forward(level):
        diag_loads[level].wait()
        terms = left_terms(jnp.concatenate(folds_of(level), axis=1))
        forward[:, wide_of(level)] = terms

    def prepare_backward(level):
        terms = left_terms(jnp.concatenate([fold.T for fold in folds_of(level)], axis=0))
        backward[tall_of(level), :] = terms

    def prepare_maps(level):
        row_ids = lax.broadcasted_iota(jnp.int32, (ROWS, MAPPED), 0)
        pair = []
        for half in range(2):
            onehot = (row_ids == maps_ref[level, half : half + 1, :]).astype(F32)
            pair.append(exact(onehot, panels_ref[level, half]))
        mats[level] = left_terms(jnp.concatenate(pair, axis=0))
        mats_t[level] = left_terms(jnp.concatenate([mat.T for mat in pair], axis=1))

    def wait_for(ref, sem):
        pltpu.make_async_copy(ref, ref, sem).wait()

    def scatter_start(stream, level):
        def step(place):
            to = peer(place)
            pltpu.make_async_remote_copy(
                src_ref=part.at[stream, level, to],
                dst_ref=rs_recv.at[stream, level, blk],
                send_sem=rs_send_sem.at[stream, level],
                recv_sem=rs_recv_sem.at[stream, level],
                device_id=device(cube, to),
                device_id_type=pl.DeviceIdType.MESH,
            ).start()

        for place in ring:
            step(place)

    def gather_start(stream, level):
        def step(place):
            to = peer(place)
            pltpu.make_async_remote_copy(
                src_ref=gather.at[stream, level, blk],
                dst_ref=gather.at[stream, level, blk],
                send_sem=ag_send_sem.at[stream, level],
                recv_sem=ag_recv_sem.at[stream, level],
                device_id=device(cube, to),
                device_id_type=pl.DeviceIdType.MESH,
            ).start()

        for place in ring:
            step(place)

    others = pl.ds(0, n_blk - 1)
    streams = range(STREAMS)

    def columns_of(stream):
        return pl.ds(stream * COLS, COLS)

    def scatter(stream, level, entry):
        products = dot(forward[:, wide_of(level)], spread_terms(entry))
        part[stream, level] = products.reshape(n_blk, SUB, LANES)
        if level == 0 and stream == 0:
            pl.semaphore_wait(barrier, n_blk + n_cube - 2)
        scatter_start(stream, level)
        rs_recv[stream, level, blk] = part[stream, level, blk]

    def climb(stream, level):
        wait_for(rs_recv.at[stream, level, others], rs_recv_sem.at[stream, level])
        solved_packed = jnp.sum(rs_recv[stream, level], axis=0)
        if level + 1 == LEVELS:
            gather[stream, level, blk] = solved_packed
            gather_start(stream, level)
            return
        solved_rows = unpack(solved_packed[None])
        solved[stream, level] = solved_rows
        width = 2**level
        reach = 2 * width
        base = cube - lax.rem(cube, reach)
        mine = lax.rem(cube, reach)
        updates = dot(mats[level], right_terms(solved_rows))
        kept = rhs_ref[level + 1, :, columns_of(stream)] - updates[:ROWS]
        given = updates[ROWS:]
        spread[stream, level, mine, 0] = pack(kept)[0]
        spread[stream, level, mine, 1] = pack(given)[0]

        def up(member):
            pltpu.make_async_remote_copy(
                src_ref=spread.at[stream, level, mine],
                dst_ref=spread.at[stream, level, mine],
                send_sem=up_send_sem.at[stream, level],
                recv_sem=up_recv_sem.at[stream, level],
                device_id=device(base + member, blk),
                device_id_type=pl.DeviceIdType.MESH,
            ).start()

        for member in members(mine, reach):
            up(member)

    def enter(stream, level):
        if level + 1 == LEVELS:
            return
        width = 2**level
        reach = 2 * width
        wait_for(
            spread.at[stream, level, pl.ds(0, reach - 1)], up_recv_sem.at[stream, level]
        )
        entry = [
            spread[stream, level, p, 0] - spread[stream, level, p ^ width, 1]
            for p in range(reach)
        ]
        scatter(stream, level + 1, jnp.stack(entry))

    def descend(stream, level):
        wait_for(gather.at[stream, level, others], ag_recv_sem.at[stream, level])
        work = gather[stream, level].reshape(n_blk * SUB, LANES)
        packed = collect_terms(
            dot(backward[tall_of(level), :], right_terms(work)), 2**level
        )
        if level == 0:
            out_ref[0, :, columns_of(stream)] = unpack(packed)
            return
        width = 2**level
        base = cube - lax.rem(cube, width)
        mine = lax.rem(cube, width)
        under = level - 1
        for p in range(width):
            sums_send[stream, under, p, 0] = packed[p]
            sums_send[stream, under, p, 1] = packed[p ^ (width // 2)]

        def down(to):
            pltpu.make_async_remote_copy(
                src_ref=sums_send.at[stream, under, to],
                dst_ref=sums_recv.at[stream, under, mine],
                send_sem=down_send_sem.at[stream, under],
                recv_sem=down_recv_sem.at[stream, under],
                device_id=device(base + to, blk),
                device_id_type=pl.DeviceIdType.MESH,
            ).start()

        for member in members(mine, width):
            down(member)
        sums_recv[stream, under, mine] = sums_send[stream, under, mine]

    def leave(stream, level):
        if level == 0:
            return
        width = 2**level
        under = level - 1
        wait_for(
            sums_recv.at[stream, under, pl.ds(0, width - 1)],
            down_recv_sem.at[stream, under],
        )
        totals = sums_recv[stream, under, 0]
        for p in range(1, width):
            totals = totals + sums_recv[stream, under, p]
        both = unpack(totals)
        left = solved[stream, under] - dot(mats_t[under], right_terms(both))
        gather[stream, under, blk] = pack(left)[0]
        gather_start(stream, under)
        out_ref[level, :, columns_of(stream)] = both[:ROWS]

    prepare_forward(0)
    rhs_load.wait()
    for stream in streams:
        scatter(stream, 0, pack(rhs_ref[0, :, columns_of(stream)]))
    def in_turn(first, second, level, interleave):
        if interleave:
            for stream in streams:
                first(stream, level)
            for stream in streams:
                second(stream, level)
        else:
            for stream in streams:
                first(stream, level)
                second(stream, level)

    panels_load.wait()
    maps_load.wait()
    prepare_maps(0)
    prepare_forward(1)
    for level in range(LEVELS):
        in_turn(climb, enter, level, UP_TURNS[level])
        if level + 2 < LEVELS:
            prepare_maps(level + 1)
            prepare_forward(level + 2)
        elif level + 2 == LEVELS:
            prepare_backward(LEVELS - 1)
            prepare_backward(LEVELS - 2)
        else:
            for below in range(LEVELS - 2):
                prepare_backward(below)
    for level in reversed(range(LEVELS)):
        in_turn(descend, leave, level, DOWN_TURNS[level])

    for stream in streams:
        for level in range(LEVELS):
            wait_for(part.at[stream, level, others], rs_send_sem.at[stream, level])
            wait_for(gather.at[stream, level, others], ag_send_sem.at[stream, level])
            if level + 1 < LEVELS:
                rest = pl.ds(0, 2 * 2**level - 1)
                wait_for(spread.at[stream, level, rest], up_send_sem.at[stream, level])
                wait_for(
                    sums_send.at[stream, level, rest], down_send_sem.at[stream, level]
                )


def body(n_cube, n_blk, right_side, diag_inverse, panels, extend_map):
    rhs = right_side[:, 0, 0]
    blocks = panels[:, 0, 0]
    maps = extend_map[:, 0, 0]
    rows, columns = diag_inverse.shape
    widest = 2 ** (LEVELS - 1)
    vmem = pl.BlockSpec(memory_space=pltpu.VMEM)
    chunks = pltpu.VMEM((STREAMS, LEVELS, n_blk, SUB, LANES), F32)
    pairs = pltpu.VMEM((STREAMS, LEVELS - 1, widest, 2, SUB, LANES), F32)
    result = pl.pallas_call(
        functools.partial(kernel, n_cube, n_blk),
        out_shape=jax.ShapeDtypeStruct(rhs.shape, F32),
        in_specs=[pl.BlockSpec(memory_space=pltpu.HBM)] * 4,
        out_specs=vmem,
        scratch_shapes=[
            pltpu.VMEM(rhs.shape, F32),
            pltpu.VMEM(diag_inverse.shape, F32),
            pltpu.VMEM(blocks.shape, F32),
            pltpu.VMEM(maps.shape, jnp.int32),
            pltpu.VMEM((n_blk * SUB, 3 * FOLD * rows), BF16),
            pltpu.VMEM((FOLD * rows, 3 * n_blk * SUB), BF16),
            pltpu.VMEM((LEVELS - 1, 2 * ROWS, 3 * ROWS), BF16),
            pltpu.VMEM((LEVELS - 1, ROWS, 6 * ROWS), BF16),
            pltpu.VMEM((STREAMS, LEVELS - 1, ROWS, COLS), F32),
            chunks,
            chunks,
            chunks,
            pairs,
            pairs,
            pairs,
        ]
        + [pltpu.SemaphoreType.DMA((STREAMS, LEVELS))] * 4
        + [pltpu.SemaphoreType.DMA((STREAMS, LEVELS - 1))] * 4
        + [pltpu.SemaphoreType.DMA((LEVELS + 3,))],
        compiler_params=pltpu.CompilerParams(
            collective_id=0, has_side_effects=True, vmem_limit_bytes=62 * 2**20
        ),
    )(rhs, diag_inverse, blocks, maps)
    return result[:, None, None]


def solution(mesh):
    placed = (
        P(None, "cube", "blk", None, None),
        P("cube", "blk"),
        P(None, "cube", "blk", None, None, None),
        P(None, "cube", "blk", None, None),
    )
    return jax.shard_map(
        functools.partial(body, mesh.shape["cube"], mesh.shape["blk"]),
        mesh=mesh,
        in_specs=placed,
        out_specs=P(None, "cube", "blk", None, None),
        check_vma=False,
    )
```

```python
import functools

import jax
import jax.numpy as jnp
from jax import lax
from jax.experimental import pallas as pl
from jax.experimental.pallas import tpu as pltpu
from jax.sharding import PartitionSpec as P

F32 = jnp.float32
BF16 = jnp.bfloat16
LEVELS = 4
ROWS = 32
MAPPED = 16
K = 64
STREAMS = 2
COLS = K // STREAMS
LANES = 128
FOLD = LANES // COLS
SUB = ROWS // FOLD
N_Y = 4
SCALE = 32.0
UP_TURNS = (False, True, True, False)
DOWN_TURNS = (False, False, True, True)


def split(value):
    high = value.astype(BF16)
    return high, (value - high.astype(F32)).astype(BF16)


def dot(a, b):
    return jnp.dot(a, b, preferred_element_type=F32)


def left_terms(value):
    high, low = split(value)
    return jnp.concatenate([high, high, low], axis=1)


def right_terms(value):
    high, low = split(value)
    return jnp.concatenate([high, low, high], axis=0)


def lane_group(shape):
    return lax.broadcasted_iota(jnp.int32, shape, len(shape) - 1) // COLS


def spread_terms(packed):
    count = packed.shape[0]
    high = packed.astype(BF16).astype(F32)
    blocks = []
    for value in (high, packed - high):
        turned = [value] + [pltpu.roll(value, COLS * i, 2) for i in range(1, FOLD)]
        block = []
        for lanes in range(FOLD):
            rows = [turned[(lanes - fold) % FOLD] for fold in range(FOLD)]
            rows = jnp.stack(rows, axis=1)
            rows = jnp.where(lane_group(rows.shape) == lanes, rows, 0.0)
            block.append(rows.reshape(count * ROWS, LANES))
        blocks.append(jnp.concatenate(block, axis=0).astype(BF16))
    return jnp.concatenate([blocks[0], blocks[1], blocks[0]], axis=0)


def collect_terms(terms, count):
    parts = terms.reshape(FOLD, count, FOLD, SUB, LANES)
    group = lane_group((count, SUB, LANES))
    total = None
    for turn in range(FOLD):
        piece = parts[0, :, turn]
        for fold in range(1, FOLD):
            piece = jnp.where(group == fold, parts[fold, :, (fold + turn) % FOLD], piece)
        if turn:
            total = total + pltpu.roll(piece, COLS * turn, 2)
        else:
            total = piece
    return total


def exact(a, b):
    return jnp.dot(a, b, precision=lax.Precision.HIGHEST, preferred_element_type=F32)


def pack(rows):
    count = rows.shape[0] // ROWS
    parts = rows.reshape(count, FOLD, SUB, COLS)
    return jnp.concatenate([parts[:, i] for i in range(FOLD)], axis=-1)


def unpack(packed):
    count = packed.shape[0]
    parts = [packed[:, :, i * COLS : (i + 1) * COLS] for i in range(FOLD)]
    return jnp.stack(parts, axis=1).reshape(count * ROWS, COLS)


def kernel(
    n_cube,
    n_blk,
    rhs_hbm,
    diag_hbm,
    panels_hbm,
    maps_hbm,
    out_ref,
    rhs_ref,
    diag_ref,
    panels_ref,
    maps_ref,
    forward,
    backward,
    correct,
    base_rows,
    facts,
    solved,
    part,
    rs_recv,
    gather,
    spread,
    sums_send,
    sums_recv,
    rows_send,
    rows_recv,
    rs_send_sem,
    rs_recv_sem,
    ag_send_sem,
    ag_recv_sem,
    up_send_sem,
    up_recv_sem,
    down_send_sem,
    down_recv_sem,
    rows_send_sem,
    rows_recv_sem,
    fact_send_sem,
    fact_recv_sem,
    load_sem,
):
    cube = lax.axis_index("cube")
    blk = lax.axis_index("blk")

    n_y = min(N_Y, n_blk)
    depth = n_blk // n_y
    plane = blk // n_y
    column = lax.rem(blk, n_y)
    ring = sorted(
        [(dz, dy) for dz in range(depth) for dy in range(n_y) if dz + dy],
        key=lambda at: -(min(at[0], depth - at[0]) + min(at[1], n_y - at[1])),
    )

    def peer(place):
        return lax.rem(plane + place[0], depth) * n_y + lax.rem(column + place[1], n_y)

    def members(mine, size):
        chips = size // 2
        order = sorted(
            [(dx, core) for dx in range(chips) for core in range(2) if dx + core],
            key=lambda at: -min(at[0], chips - at[0]),
        )
        return [
            lax.rem(mine // 2 + dx, chips) * 2 + lax.rem(lax.rem(mine, 2) + core, 2)
            for dx, core in order
        ]

    def device(c, b):
        return {"cube": c, "blk": b}

    def rows_of(level):
        return pl.ds((2**level - 1) * ROWS, 2**level * ROWS)

    diag_loads = [
        pltpu.make_async_copy(
            diag_hbm.at[rows_of(level), :],
            diag_ref.at[rows_of(level), :],
            load_sem.at[level],
        )
        for level in range(LEVELS)
    ]
    rhs_load = pltpu.make_async_copy(rhs_hbm, rhs_ref, load_sem.at[LEVELS])
    panels_load = pltpu.make_async_copy(panels_hbm, panels_ref, load_sem.at[LEVELS + 1])
    maps_load = pltpu.make_async_copy(maps_hbm, maps_ref, load_sem.at[LEVELS + 2])
    diag_loads[0].start()
    rhs_load.start()
    panels_load.start()
    maps_load.start()
    for load in diag_loads[1:]:
        load.start()

    barrier = pltpu.get_barrier_semaphore()

    def greet_blk(step, carry):
        pl.semaphore_signal(
            barrier, inc=1, device_id=device(cube, lax.rem(blk + step, n_blk)),
            device_id_type=pl.DeviceIdType.MESH,
        )
        return carry

    def greet_cube(step, carry):
        pl.semaphore_signal(
            barrier, inc=1, device_id=device(lax.rem(cube + step, n_cube), blk),
            device_id_type=pl.DeviceIdType.MESH,
        )
        return carry

    lax.fori_loop(1, n_blk, greet_blk, 0)
    lax.fori_loop(1, n_cube, greet_cube, 0)

    def wide_of(level):
        return slice(3 * FOLD * (2**level - 1) * ROWS, 3 * FOLD * (2**(level + 1) - 1) * ROWS)

    def tall_of(level):
        return slice(FOLD * (2**level - 1) * ROWS, FOLD * (2**(level + 1) - 1) * ROWS)

    def folds_of(level):
        columns = diag_ref[rows_of(level), :].T
        span = columns.shape[1]
        parts = columns.reshape(n_blk, FOLD, SUB, span)
        return [parts[:, i].reshape(n_blk * SUB, span) for i in range(FOLD)]

    def beside(folds):
        return left_terms(jnp.concatenate(folds, axis=1))

    def below(folds):
        return left_terms(jnp.concatenate([fold.T for fold in folds], axis=0))

    def prepare_facts(level):
        reach = 2 * 2**level
        mine = lax.rem(cube, reach)
        row_ids = lax.broadcasted_iota(jnp.int32, (ROWS, MAPPED), 0)
        for half in range(2):
            onehot = (row_ids == maps_ref[level, half : half + 1, :]).astype(F32)
            mat = exact(onehot, panels_ref[level, half]) * (-1.0 / SCALE)
            facts[level, mine, half] = pack(mat)[0]
        for stream in range(STREAMS):
            rows = rhs_ref[level + 1, :, columns_of(stream)]
            facts[level, mine, 2 + stream] = pack(rows)[0]

    def exchange_facts(level):
        reach = 2 * 2**level
        base = cube - lax.rem(cube, reach)
        mine = lax.rem(cube, reach)
        for member in members(mine, reach):
            pltpu.make_async_remote_copy(
                src_ref=facts.at[level, mine],
                dst_ref=facts.at[level, mine],
                send_sem=fact_send_sem.at[level],
                recv_sem=fact_recv_sem.at[level],
                device_id=device(base + member, blk),
                device_id_type=pl.DeviceIdType.MESH,
            ).start()

    def combine(under):
        level = under + 1
        width = 2**under
        reach = 2 * width
        diag_loads[level].wait()
        wait_for(facts.at[under, pl.ds(0, reach - 1)], fact_recv_sem.at[under])
        zero = jnp.zeros((ROWS, ROWS), F32)
        lines = []
        for p in range(reach):
            line = [zero] * reach
            line[p] = unpack(facts[under, p, 0][None])
            line[p ^ width] = unpack(facts[under, p ^ width, 1][None])
            lines.append(jnp.concatenate(line, axis=1))
        update = jnp.concatenate(lines, axis=0)
        folds = folds_of(level)
        stacked = exact(jnp.concatenate(folds, axis=0), update)
        height = n_blk * SUB
        merged = [stacked[i * height : (i + 1) * height] for i in range(FOLD)]
        forward[:, wide_of(level)] = beside(merged)
        correct[tall_of(level), :] = below(merged)
        plain = beside(folds)
        for stream in range(STREAMS):
            rows = jnp.stack([facts[under, p, 2 + stream] for p in range(reach)])
            base_rows[stream, under] = dot(plain, spread_terms(rows))

    def prepare_backward(level):
        backward[tall_of(level), :] = below(folds_of(level))

    def wait_for(ref, sem):
        pltpu.make_async_copy(ref, ref, sem).wait()

    def scatter_start(stream, level):
        def step(place):
            to = peer(place)
            pltpu.make_async_remote_copy(
                src_ref=part.at[stream, level, to],
                dst_ref=rs_recv.at[stream, level, blk],
                send_sem=rs_send_sem.at[stream, level],
                recv_sem=rs_recv_sem.at[stream, level],
                device_id=device(cube, to),
                device_id_type=pl.DeviceIdType.MESH,
            ).start()

        for place in ring:
            step(place)

    def gather_start(stream, level):
        def step(place):
            to = peer(place)
            pltpu.make_async_remote_copy(
                src_ref=gather.at[stream, level, blk],
                dst_ref=gather.at[stream, level, blk],
                send_sem=ag_send_sem.at[stream, level],
                recv_sem=ag_recv_sem.at[stream, level],
                device_id=device(cube, to),
                device_id_type=pl.DeviceIdType.MESH,
            ).start()

        for place in ring:
            step(place)

    others = pl.ds(0, n_blk - 1)
    streams = range(STREAMS)

    def columns_of(stream):
        return pl.ds(stream * COLS, COLS)

    def scatter(stream, level, entry):
        products = dot(forward[:, wide_of(level)], spread_terms(entry))
        if level:
            products = base_rows[stream, level - 1] + SCALE * products
        part[stream, level] = products.reshape(n_blk, SUB, LANES)
        if level == 0 and stream == 0:
            pl.semaphore_wait(barrier, n_blk + n_cube - 2)
        scatter_start(stream, level)
        rs_recv[stream, level, blk] = part[stream, level, blk]

    def climb(stream, level):
        wait_for(rs_recv.at[stream, level, others], rs_recv_sem.at[stream, level])
        rows = jnp.sum(rs_recv[stream, level], axis=0)
        if level + 1 == LEVELS:
            gather[stream, level, blk] = rows
            gather_start(stream, level)
            return
        reach = 2 * 2**level
        base = cube - lax.rem(cube, reach)
        mine = lax.rem(cube, reach)
        spread[stream, level, mine] = rows
        for member in members(mine, reach):
            pltpu.make_async_remote_copy(
                src_ref=spread.at[stream, level, mine],
                dst_ref=spread.at[stream, level, mine],
                send_sem=up_send_sem.at[stream, level],
                recv_sem=up_recv_sem.at[stream, level],
                device_id=device(base + member, blk),
                device_id_type=pl.DeviceIdType.MESH,
            ).start()
        solved[stream, level] = rows

    def enter(stream, level):
        if level + 1 == LEVELS:
            return
        reach = 2 * 2**level
        wait_for(
            spread.at[stream, level, pl.ds(0, reach - 1)], up_recv_sem.at[stream, level]
        )
        scatter(stream, level + 1, spread[stream, level, :reach])

    def send_down(stream, level, source, target, send_sem, recv_sem):
        width = 2**level
        under = level - 1
        base = cube - lax.rem(cube, width)
        mine = lax.rem(cube, width)
        for member in members(mine, width):
            pltpu.make_async_remote_copy(
                src_ref=source.at[stream, under, member],
                dst_ref=target.at[stream, under, mine],
                send_sem=send_sem.at[stream, under],
                recv_sem=recv_sem.at[stream, under],
                device_id=device(base + member, blk),
                device_id_type=pl.DeviceIdType.MESH,
            ).start()
        target[stream, under, mine] = source[stream, under, mine]

    def receive_down(stream, level, target, recv_sem):
        width = 2**level
        under = level - 1
        wait_for(
            target.at[stream, under, pl.ds(0, width - 1)], recv_sem.at[stream, under]
        )
        return jnp.sum(target[stream, under, :width], axis=0)

    def descend(stream, level):
        width = 2**level
        wait_for(gather.at[stream, level, others], ag_recv_sem.at[stream, level])
        work = right_terms(gather[stream, level].reshape(n_blk * SUB, LANES))
        if level:
            sums = collect_terms(dot(correct[tall_of(level), :], work), width)
            sums_send[stream, level - 1, :width] = sums
            send_down(stream, level, sums_send, sums_recv, down_send_sem, down_recv_sem)
        rows = collect_terms(dot(backward[tall_of(level), :], work), width)
        if level:
            rows_send[stream, level - 1, :width] = rows
            send_down(stream, level, rows_send, rows_recv, rows_send_sem, rows_recv_sem)
        else:
            out_ref[0, :, columns_of(stream)] = unpack(rows)

    def leave(stream, level):
        if level == 0:
            return
        under = level - 1
        sums = receive_down(stream, level, sums_recv, down_recv_sem)
        gather[stream, under, blk] = solved[stream, under] + SCALE * sums
        gather_start(stream, under)

    def finish(stream, level):
        if level:
            rows = receive_down(stream, level, rows_recv, rows_recv_sem)
            out_ref[level, :, columns_of(stream)] = unpack(rows[None])

    diag_loads[0].wait()
    forward[:, wide_of(0)] = beside(folds_of(0))
    rhs_load.wait()
    for stream in streams:
        scatter(stream, 0, pack(rhs_ref[0, :, columns_of(stream)]))
        if stream == 0:
            panels_load.wait()
            maps_load.wait()
            for level in range(LEVELS - 1):
                prepare_facts(level)
                exchange_facts(level)
    combine(0)

    def in_turn(first, second, level, interleave):
        if interleave:
            for stream in streams:
                first(stream, level)
            for stream in streams:
                second(stream, level)
        else:
            for stream in streams:
                first(stream, level)
                second(stream, level)

    for level in range(LEVELS):
        in_turn(climb, enter, level, UP_TURNS[level])
        if level + 2 < LEVELS:
            combine(level + 1)
        elif level + 2 == LEVELS:
            prepare_backward(LEVELS - 1)
            prepare_backward(LEVELS - 2)
        else:
            for low in range(LEVELS - 2):
                prepare_backward(low)
    for level in reversed(range(LEVELS)):
        in_turn(descend, leave, level, DOWN_TURNS[level])
        for stream in streams:
            finish(stream, level)

    for level in range(LEVELS - 1):
        rest = pl.ds(0, 2 * 2**level - 1)
        wait_for(facts.at[level, rest], fact_send_sem.at[level])
    for stream in streams:
        for level in range(LEVELS):
            wait_for(part.at[stream, level, others], rs_send_sem.at[stream, level])
            wait_for(gather.at[stream, level, others], ag_send_sem.at[stream, level])
            if level + 1 < LEVELS:
                rest = pl.ds(0, 2 * 2**level - 1)
                wait_for(spread.at[stream, level, rest], up_send_sem.at[stream, level])
                wait_for(
                    sums_send.at[stream, level, rest], down_send_sem.at[stream, level]
                )
                wait_for(
                    rows_send.at[stream, level, rest], rows_send_sem.at[stream, level]
                )


def body(n_cube, n_blk, right_side, diag_inverse, panels, extend_map):
    rhs = right_side[:, 0, 0]
    blocks = panels[:, 0, 0]
    maps = extend_map[:, 0, 0]
    rows, columns = diag_inverse.shape
    widest = 2 ** (LEVELS - 1)
    vmem = pl.BlockSpec(memory_space=pltpu.VMEM)
    chunks = pltpu.VMEM((STREAMS, LEVELS, n_blk, SUB, LANES), F32)
    sets = pltpu.VMEM((STREAMS, LEVELS - 1, widest, SUB, LANES), F32)
    result = pl.pallas_call(
        functools.partial(kernel, n_cube, n_blk),
        out_shape=jax.ShapeDtypeStruct(rhs.shape, F32),
        in_specs=[pl.BlockSpec(memory_space=pltpu.HBM)] * 4,
        out_specs=vmem,
        scratch_shapes=[
            pltpu.VMEM(rhs.shape, F32),
            pltpu.VMEM(diag_inverse.shape, F32),
            pltpu.VMEM(blocks.shape, F32),
            pltpu.VMEM(maps.shape, jnp.int32),
            pltpu.VMEM((n_blk * SUB, 3 * FOLD * rows), BF16),
            pltpu.VMEM((FOLD * rows, 3 * n_blk * SUB), BF16),
            pltpu.VMEM((FOLD * rows, 3 * n_blk * SUB), BF16),
            pltpu.VMEM((STREAMS, LEVELS - 1, n_blk * SUB, LANES), F32),
            pltpu.VMEM((LEVELS - 1, widest, 2 + STREAMS, SUB, LANES), F32),
            pltpu.VMEM((STREAMS, LEVELS - 1, SUB, LANES), F32),
            chunks,
            chunks,
            chunks,
            sets,
            sets,
            sets,
            sets,
            sets,
        ]
        + [pltpu.SemaphoreType.DMA((STREAMS, LEVELS))] * 4
        + [pltpu.SemaphoreType.DMA((STREAMS, LEVELS - 1))] * 6
        + [pltpu.SemaphoreType.DMA((LEVELS - 1,))] * 2
        + [pltpu.SemaphoreType.DMA((LEVELS + 3,))],
        compiler_params=pltpu.CompilerParams(
            collective_id=0, has_side_effects=True, vmem_limit_bytes=62 * 2**20
        ),
    )(rhs, diag_inverse, blocks, maps)
    return result[:, None, None]


def solution(mesh):
    placed = (
        P(None, "cube", "blk", None, None),
        P("cube", "blk"),
        P(None, "cube", "blk", None, None, None),
        P(None, "cube", "blk", None, None),
    )
    return jax.shard_map(
        functools.partial(body, mesh.shape["cube"], mesh.shape["blk"]),
        mesh=mesh,
        in_specs=placed,
        out_specs=P(None, "cube", "blk", None, None),
        check_vma=False,
    )
```

```python
import functools

import jax
import jax.numpy as jnp
from jax import lax
from jax.experimental import pallas as pl
from jax.experimental.pallas import tpu as pltpu
from jax.sharding import PartitionSpec as P

F32 = jnp.float32
BF16 = jnp.bfloat16
LEVELS = 4
ROWS = 32
MAPPED = 16
K = 64
STREAMS = 2
COLS = K // STREAMS
LANES = 128
FOLD = LANES // COLS
SUB = ROWS // FOLD
N_Y = 4
SCALE = 32.0
UP_TURNS = (False, True, True, False)
DOWN_TURNS = (False, False, True, True)


def split(value):
    high = value.astype(BF16)
    return high, (value - high.astype(F32)).astype(BF16)


def dot(a, b):
    return jnp.dot(a, b, preferred_element_type=F32)


def left_terms(value):
    high, low = split(value)
    return jnp.concatenate([high, high, low], axis=1)


def right_terms(value):
    high, low = split(value)
    return jnp.concatenate([high, low, high], axis=0)


def lane_group(shape):
    return lax.broadcasted_iota(jnp.int32, shape, len(shape) - 1) // COLS


def spread_terms(packed):
    count = packed.shape[0]
    high = packed.astype(BF16).astype(F32)
    blocks = []
    for value in (high, packed - high):
        turned = [value] + [pltpu.roll(value, COLS * i, 2) for i in range(1, FOLD)]
        block = []
        for lanes in range(FOLD):
            rows = [turned[(lanes - fold) % FOLD] for fold in range(FOLD)]
            rows = jnp.stack(rows, axis=1)
            rows = jnp.where(lane_group(rows.shape) == lanes, rows, 0.0)
            block.append(rows.reshape(count * ROWS, LANES))
        blocks.append(jnp.concatenate(block, axis=0).astype(BF16))
    return jnp.concatenate([blocks[0], blocks[1], blocks[0]], axis=0)


def collect_terms(terms, count):
    parts = terms.reshape(FOLD, count, FOLD, SUB, LANES)
    group = lane_group((count, SUB, LANES))
    total = None
    for turn in range(FOLD):
        piece = parts[0, :, turn]
        for fold in range(1, FOLD):
            piece = jnp.where(group == fold, parts[fold, :, (fold + turn) % FOLD], piece)
        if turn:
            total = total + pltpu.roll(piece, COLS * turn, 2)
        else:
            total = piece
    return total


def exact(a, b):
    return jnp.dot(a, b, precision=lax.Precision.HIGHEST, preferred_element_type=F32)


def pack(rows):
    count = rows.shape[0] // ROWS
    parts = rows.reshape(count, FOLD, SUB, COLS)
    return jnp.concatenate([parts[:, i] for i in range(FOLD)], axis=-1)


def unpack(packed):
    count = packed.shape[0]
    parts = [packed[:, :, i * COLS : (i + 1) * COLS] for i in range(FOLD)]
    return jnp.stack(parts, axis=1).reshape(count * ROWS, COLS)


def kernel(
    n_cube,
    n_blk,
    rhs_hbm,
    diag_hbm,
    panels_hbm,
    maps_hbm,
    out_ref,
    rhs_ref,
    diag_ref,
    panels_ref,
    maps_ref,
    forward,
    backward,
    correct,
    base_rows,
    facts,
    solved,
    part,
    rs_recv,
    gather,
    spread,
    sums_send,
    sums_recv,
    rows_send,
    rows_recv,
    rs_send_sem,
    rs_recv_sem,
    ag_send_sem,
    ag_recv_sem,
    up_send_sem,
    up_recv_sem,
    down_send_sem,
    down_recv_sem,
    rows_send_sem,
    rows_recv_sem,
    fact_send_sem,
    fact_recv_sem,
    load_sem,
):
    cube = lax.axis_index("cube")
    blk = lax.axis_index("blk")

    n_y = min(N_Y, n_blk)
    depth = n_blk // n_y
    plane = blk // n_y
    column = lax.rem(blk, n_y)
    ring = sorted(
        [(dz, dy) for dz in range(depth) for dy in range(n_y) if dz + dy],
        key=lambda at: -(min(at[0], depth - at[0]) + 2 * min(at[1], n_y - at[1])),
    )

    def peer(place):
        return lax.rem(plane + place[0], depth) * n_y + lax.rem(column + place[1], n_y)

    def members(mine, size):
        chips = size // 2
        order = sorted(
            [(dx, core) for dx in range(chips) for core in range(2) if dx + core],
            key=lambda at: -min(at[0], chips - at[0]),
        )
        return [
            lax.rem(mine // 2 + dx, chips) * 2 + lax.rem(lax.rem(mine, 2) + core, 2)
            for dx, core in order
        ]

    def device(c, b):
        return {"cube": c, "blk": b}

    def rows_of(level):
        return pl.ds((2**level - 1) * ROWS, 2**level * ROWS)

    diag_loads = [
        pltpu.make_async_copy(
            diag_hbm.at[rows_of(level), :],
            diag_ref.at[rows_of(level), :],
            load_sem.at[level],
        )
        for level in range(LEVELS)
    ]
    rhs_load = pltpu.make_async_copy(rhs_hbm, rhs_ref, load_sem.at[LEVELS])
    panels_load = pltpu.make_async_copy(panels_hbm, panels_ref, load_sem.at[LEVELS + 1])
    maps_load = pltpu.make_async_copy(maps_hbm, maps_ref, load_sem.at[LEVELS + 2])
    barrier = pltpu.get_barrier_semaphore()

    def greet(target):
        pl.semaphore_signal(
            barrier, inc=1, device_id=target, device_id_type=pl.DeviceIdType.MESH
        )

    for place in ring:
        greet(device(cube, peer(place)))
    for member in members(cube, n_cube):
        greet(device(member, blk))
    diag_loads[0].start()
    rhs_load.start()
    panels_load.start()
    maps_load.start()
    for load in diag_loads[1:]:
        load.start()

    def wide_of(level):
        return slice(3 * FOLD * (2**level - 1) * ROWS, 3 * FOLD * (2**(level + 1) - 1) * ROWS)

    def tall_of(level):
        return slice(FOLD * (2**level - 1) * ROWS, FOLD * (2**(level + 1) - 1) * ROWS)

    def folds_of(level):
        columns = diag_ref[rows_of(level), :].T
        span = columns.shape[1]
        parts = columns.reshape(n_blk, FOLD, SUB, span)
        return [parts[:, i].reshape(n_blk * SUB, span) for i in range(FOLD)]

    def beside(folds):
        return left_terms(jnp.concatenate(folds, axis=1))

    def below(folds):
        return left_terms(jnp.concatenate([fold.T for fold in folds], axis=0))

    def prepare_facts(level):
        reach = 2 * 2**level
        mine = lax.rem(cube, reach)
        row_ids = lax.broadcasted_iota(jnp.int32, (ROWS, MAPPED), 0)
        for half in range(2):
            onehot = (row_ids == maps_ref[level, half : half + 1, :]).astype(F32)
            mat = exact(onehot, panels_ref[level, half]) * (-1.0 / SCALE)
            facts[level, mine, half] = pack(mat)[0]
        for stream in range(STREAMS):
            rows = rhs_ref[level + 1, :, columns_of(stream)]
            facts[level, mine, 2 + stream] = pack(rows)[0]

    def exchange_facts(level):
        reach = 2 * 2**level
        base = cube - lax.rem(cube, reach)
        mine = lax.rem(cube, reach)
        for member in members(mine, reach):
            pltpu.make_async_remote_copy(
                src_ref=facts.at[level, mine],
                dst_ref=facts.at[level, mine],
                send_sem=fact_send_sem.at[level],
                recv_sem=fact_recv_sem.at[level],
                device_id=device(base + member, blk),
                device_id_type=pl.DeviceIdType.MESH,
            ).start()

    def combine(under):
        level = under + 1
        width = 2**under
        reach = 2 * width
        diag_loads[level].wait()
        wait_for(facts.at[under, pl.ds(0, reach - 1)], fact_recv_sem.at[under])
        zero = jnp.zeros((ROWS, ROWS), F32)
        lines = []
        for p in range(reach):
            line = [zero] * reach
            line[p] = unpack(facts[under, p, 0][None])
            line[p ^ width] = unpack(facts[under, p ^ width, 1][None])
            lines.append(jnp.concatenate(line, axis=1))
        update = jnp.concatenate(lines, axis=0)
        folds = folds_of(level)
        stacked = exact(jnp.concatenate(folds, axis=0), update)
        height = n_blk * SUB
        merged = [stacked[i * height : (i + 1) * height] for i in range(FOLD)]
        forward[:, wide_of(level)] = beside(merged)
        correct[tall_of(level), :] = below(merged)
        plain = beside(folds)
        for stream in range(STREAMS):
            rows = jnp.stack([facts[under, p, 2 + stream] for p in range(reach)])
            base_rows[stream, under] = dot(plain, spread_terms(rows))

    def prepare_backward(level):
        backward[tall_of(level), :] = below(folds_of(level))

    def wait_for(ref, sem):
        pltpu.make_async_copy(ref, ref, sem).wait()

    def scatter_start(stream, level):
        def step(place):
            to = peer(place)
            pltpu.make_async_remote_copy(
                src_ref=part.at[stream, level, to],
                dst_ref=rs_recv.at[stream, level, blk],
                send_sem=rs_send_sem.at[stream, level],
                recv_sem=rs_recv_sem.at[stream, level],
                device_id=device(cube, to),
                device_id_type=pl.DeviceIdType.MESH,
            ).start()

        for place in ring:
            step(place)

    def gather_start(stream, level):
        def step(place):
            to = peer(place)
            pltpu.make_async_remote_copy(
                src_ref=gather.at[stream, level, blk],
                dst_ref=gather.at[stream, level, blk],
                send_sem=ag_send_sem.at[stream, level],
                recv_sem=ag_recv_sem.at[stream, level],
                device_id=device(cube, to),
                device_id_type=pl.DeviceIdType.MESH,
            ).start()

        for place in ring:
            step(place)

    others = pl.ds(0, n_blk - 1)
    streams = range(STREAMS)

    def columns_of(stream):
        return pl.ds(stream * COLS, COLS)

    def scatter(stream, level, entry):
        products = dot(forward[:, wide_of(level)], spread_terms(entry))
        if level:
            products = base_rows[stream, level - 1] + SCALE * products
        part[stream, level] = products.reshape(n_blk, SUB, LANES)
        if level == 0 and stream == 0:
            pl.semaphore_wait(barrier, n_blk + n_cube - 2)
        scatter_start(stream, level)
        rs_recv[stream, level, blk] = part[stream, level, blk]

    def climb(stream, level):
        wait_for(rs_recv.at[stream, level, others], rs_recv_sem.at[stream, level])
        rows = jnp.sum(rs_recv[stream, level], axis=0)
        if level + 1 == LEVELS:
            gather[stream, level, blk] = rows
            gather_start(stream, level)
            return
        reach = 2 * 2**level
        base = cube - lax.rem(cube, reach)
        mine = lax.rem(cube, reach)
        spread[stream, level, mine] = rows
        for member in members(mine, reach):
            pltpu.make_async_remote_copy(
                src_ref=spread.at[stream, level, mine],
                dst_ref=spread.at[stream, level, mine],
                send_sem=up_send_sem.at[stream, level],
                recv_sem=up_recv_sem.at[stream, level],
                device_id=device(base + member, blk),
                device_id_type=pl.DeviceIdType.MESH,
            ).start()
        solved[stream, level] = rows

    def enter(stream, level):
        if level + 1 == LEVELS:
            return
        reach = 2 * 2**level
        wait_for(
            spread.at[stream, level, pl.ds(0, reach - 1)], up_recv_sem.at[stream, level]
        )
        scatter(stream, level + 1, spread[stream, level, :reach])

    def send_down(stream, level, source, target, send_sem, recv_sem):
        width = 2**level
        under = level - 1
        base = cube - lax.rem(cube, width)
        mine = lax.rem(cube, width)
        for member in members(mine, width):
            pltpu.make_async_remote_copy(
                src_ref=source.at[stream, under, member],
                dst_ref=target.at[stream, under, mine],
                send_sem=send_sem.at[stream, under],
                recv_sem=recv_sem.at[stream, under],
                device_id=device(base + member, blk),
                device_id_type=pl.DeviceIdType.MESH,
            ).start()
        target[stream, under, mine] = source[stream, under, mine]

    def receive_down(stream, level, target, recv_sem):
        width = 2**level
        under = level - 1
        wait_for(
            target.at[stream, under, pl.ds(0, width - 1)], recv_sem.at[stream, under]
        )
        return jnp.sum(target[stream, under, :width], axis=0)

    def descend(stream, level):
        width = 2**level
        wait_for(gather.at[stream, level, others], ag_recv_sem.at[stream, level])
        work = right_terms(gather[stream, level].reshape(n_blk * SUB, LANES))
        if level:
            sums = collect_terms(dot(correct[tall_of(level), :], work), width)
            sums_send[stream, level - 1, :width] = sums
            send_down(stream, level, sums_send, sums_recv, down_send_sem, down_recv_sem)
        rows = collect_terms(dot(backward[tall_of(level), :], work), width)
        if level:
            rows_send[stream, level - 1, :width] = rows
            send_down(stream, level, rows_send, rows_recv, rows_send_sem, rows_recv_sem)
        else:
            out_ref[0, :, columns_of(stream)] = unpack(rows)

    def leave(stream, level):
        if level == 0:
            return
        under = level - 1
        sums = receive_down(stream, level, sums_recv, down_recv_sem)
        gather[stream, under, blk] = solved[stream, under] + SCALE * sums
        gather_start(stream, under)

    def finish(stream, level):
        if level:
            rows = receive_down(stream, level, rows_recv, rows_recv_sem)
            out_ref[level, :, columns_of(stream)] = unpack(rows[None])

    diag_loads[0].wait()
    forward[:, wide_of(0)] = beside(folds_of(0))
    rhs_load.wait()
    for stream in streams:
        scatter(stream, 0, pack(rhs_ref[0, :, columns_of(stream)]))
        if stream == 0:
            panels_load.wait()
            maps_load.wait()
            for level in range(LEVELS - 1):
                prepare_facts(level)
                exchange_facts(level)
    combine(0)

    def in_turn(first, second, level, interleave):
        if interleave:
            for stream in streams:
                first(stream, level)
            for stream in streams:
                second(stream, level)
        else:
            for stream in streams:
                first(stream, level)
                second(stream, level)

    def drain_up(level):
        for stream in streams:
            wait_for(part.at[stream, level, others], rs_send_sem.at[stream, level])
            if level + 1 < LEVELS:
                rest = pl.ds(0, 2 * 2**level - 1)
                wait_for(spread.at[stream, level, rest], up_send_sem.at[stream, level])
        if level + 1 < LEVELS:
            wait_for(facts.at[level, rest], fact_send_sem.at[level])

    def drain_down(level):
        rest = pl.ds(0, 2**level - 1)
        for stream in streams:
            wait_for(gather.at[stream, level, others], ag_send_sem.at[stream, level])
            for source, sem in ((sums_send, down_send_sem), (rows_send, rows_send_sem)):
                wait_for(source.at[stream, level - 1, rest], sem.at[stream, level - 1])

    for level in range(LEVELS):
        in_turn(climb, enter, level, UP_TURNS[level])
        drain_up(level)
        if level + 2 < LEVELS:
            combine(level + 1)
        elif level + 2 == LEVELS:
            prepare_backward(LEVELS - 1)
            prepare_backward(LEVELS - 2)
        else:
            for low in range(LEVELS - 2):
                prepare_backward(low)
    for level in reversed(range(LEVELS)):
        in_turn(descend, leave, level, DOWN_TURNS[level])
        if level:
            for stream in streams:
                finish(stream, level)
            drain_down(level)

    for stream in streams:
        wait_for(gather.at[stream, 0, others], ag_send_sem.at[stream, 0])


def body(n_cube, n_blk, right_side, diag_inverse, panels, extend_map):
    rhs = right_side[:, 0, 0]
    blocks = panels[:, 0, 0]
    maps = extend_map[:, 0, 0]
    rows, columns = diag_inverse.shape
    widest = 2 ** (LEVELS - 1)
    vmem = pl.BlockSpec(memory_space=pltpu.VMEM)
    chunks = pltpu.VMEM((STREAMS, LEVELS, n_blk, SUB, LANES), F32)
    sets = pltpu.VMEM((STREAMS, LEVELS - 1, widest, SUB, LANES), F32)
    result = pl.pallas_call(
        functools.partial(kernel, n_cube, n_blk),
        out_shape=jax.ShapeDtypeStruct(rhs.shape, F32),
        in_specs=[pl.BlockSpec(memory_space=pltpu.HBM)] * 4,
        out_specs=vmem,
        scratch_shapes=[
            pltpu.VMEM(rhs.shape, F32),
            pltpu.VMEM(diag_inverse.shape, F32),
            pltpu.VMEM(blocks.shape, F32),
            pltpu.VMEM(maps.shape, jnp.int32),
            pltpu.VMEM((n_blk * SUB, 3 * FOLD * rows), BF16),
            pltpu.VMEM((FOLD * rows, 3 * n_blk * SUB), BF16),
            pltpu.VMEM((FOLD * rows, 3 * n_blk * SUB), BF16),
            pltpu.VMEM((STREAMS, LEVELS - 1, n_blk * SUB, LANES), F32),
            pltpu.VMEM((LEVELS - 1, widest, 2 + STREAMS, SUB, LANES), F32),
            pltpu.VMEM((STREAMS, LEVELS - 1, SUB, LANES), F32),
            chunks,
            chunks,
            chunks,
            sets,
            sets,
            sets,
            sets,
            sets,
        ]
        + [pltpu.SemaphoreType.DMA((STREAMS, LEVELS))] * 4
        + [pltpu.SemaphoreType.DMA((STREAMS, LEVELS - 1))] * 6
        + [pltpu.SemaphoreType.DMA((LEVELS - 1,))] * 2
        + [pltpu.SemaphoreType.DMA((LEVELS + 3,))],
        compiler_params=pltpu.CompilerParams(
            collective_id=0, has_side_effects=True, vmem_limit_bytes=40 * 2**20
        ),
    )(*[pltpu.with_memory_space_constraint(x, pltpu.HBM) for x in (rhs, diag_inverse, blocks, maps)])
    return result[:, None, None]


def solution(mesh):
    placed = (
        P(None, "cube", "blk", None, None),
        P("cube", "blk"),
        P(None, "cube", "blk", None, None, None),
        P(None, "cube", "blk", None, None),
    )
    return jax.shard_map(
        functools.partial(body, mesh.shape["cube"], mesh.shape["blk"]),
        mesh=mesh,
        in_specs=placed,
        out_specs=P(None, "cube", "blk", None, None),
        check_vma=False,
    )
```

```python
import functools

import jax
import jax.numpy as jnp
from jax import lax
from jax.experimental import pallas as pl
from jax.experimental.pallas import tpu as pltpu
from jax.sharding import PartitionSpec as P

F32 = jnp.float32
BF16 = jnp.bfloat16
LEVELS = 4
ROWS = 32
MAPPED = 16
K = 64
STREAMS = 2
COLS = K // STREAMS
LANES = 128
FOLD = LANES // COLS
SUB = ROWS // FOLD
N_Y = 4
SCALE = 32.0
UP_TURNS = (False, True, True, False)
DOWN_TURNS = (False, False, True, True)


def split(value):
    high = value.astype(BF16)
    return high, (value - high.astype(F32)).astype(BF16)


def dot(a, b):
    return jnp.dot(a, b, preferred_element_type=F32)


def left_terms(value):
    high, low = split(value)
    return jnp.concatenate([high, high, low], axis=1)


def right_terms(value):
    high, low = split(value)
    return jnp.concatenate([high, low, high], axis=0)


def lane_group(shape):
    return lax.broadcasted_iota(jnp.int32, shape, len(shape) - 1) // COLS


def spread_terms(packed):
    count = packed.shape[0]
    high = packed.astype(BF16).astype(F32)
    blocks = []
    for value in (high, packed - high):
        turned = [value] + [pltpu.roll(value, COLS * i, 2) for i in range(1, FOLD)]
        block = []
        for lanes in range(FOLD):
            rows = [turned[(lanes - fold) % FOLD] for fold in range(FOLD)]
            rows = jnp.stack(rows, axis=1)
            rows = jnp.where(lane_group(rows.shape) == lanes, rows, 0.0)
            block.append(rows.reshape(count * ROWS, LANES))
        blocks.append(jnp.concatenate(block, axis=0).astype(BF16))
    return jnp.concatenate([blocks[0], blocks[1], blocks[0]], axis=0)


def collect_terms(terms, count):
    parts = terms.reshape(FOLD, count, FOLD, SUB, LANES)
    group = lane_group((count, SUB, LANES))
    total = None
    for turn in range(FOLD):
        piece = parts[0, :, turn]
        for fold in range(1, FOLD):
            piece = jnp.where(group == fold, parts[fold, :, (fold + turn) % FOLD], piece)
        if turn:
            total = total + pltpu.roll(piece, COLS * turn, 2)
        else:
            total = piece
    return total


def exact(a, b):
    return jnp.dot(a, b, precision=lax.Precision.HIGHEST, preferred_element_type=F32)


def pack(rows):
    count = rows.shape[0] // ROWS
    parts = rows.reshape(count, FOLD, SUB, COLS)
    return jnp.concatenate([parts[:, i] for i in range(FOLD)], axis=-1)


def unpack(packed):
    count = packed.shape[0]
    parts = [packed[:, :, i * COLS : (i + 1) * COLS] for i in range(FOLD)]
    return jnp.stack(parts, axis=1).reshape(count * ROWS, COLS)


def kernel(
    n_cube,
    n_blk,
    rhs_hbm,
    diag_hbm,
    panels_hbm,
    maps_hbm,
    out_ref,
    rhs_ref,
    diag_ref,
    panels_ref,
    maps_ref,
    forward,
    backward,
    correct,
    base_rows,
    facts,
    solved,
    part,
    rs_recv,
    gather,
    spread,
    sums_send,
    sums_recv,
    rows_send,
    rows_recv,
    rs_send_sem,
    rs_recv_sem,
    ag_send_sem,
    ag_recv_sem,
    up_send_sem,
    up_recv_sem,
    down_send_sem,
    down_recv_sem,
    rows_send_sem,
    rows_recv_sem,
    fact_send_sem,
    fact_recv_sem,
    load_sem,
):
    cube = lax.axis_index("cube")
    blk = lax.axis_index("blk")

    n_y = min(N_Y, n_blk)
    depth = n_blk // n_y
    plane = blk // n_y
    column = lax.rem(blk, n_y)
    ring = sorted(
        [(dz, dy) for dz in range(depth) for dy in range(n_y) if dz + dy],
        key=lambda at: -(min(at[0], depth - at[0]) + 2 * min(at[1], n_y - at[1])),
    )

    halves = [
        [dz for dz in range(depth) if (min(dz, depth - dz) >= depth // 4) == far]
        for far in (True, False)
    ]
    halves = [half for half in halves if half]

    def peer(place):
        return lax.rem(plane + place[0], depth) * n_y + lax.rem(column + place[1], n_y)

    def members(mine, size):
        chips = size // 2
        order = sorted(
            [(dx, core) for dx in range(chips) for core in range(2) if dx + core],
            key=lambda at: -min(at[0], chips - at[0]),
        )
        return [
            lax.rem(mine // 2 + dx, chips) * 2 + lax.rem(lax.rem(mine, 2) + core, 2)
            for dx, core in order
        ]

    def device(c, b):
        return {"cube": c, "blk": b}

    def rows_of(level):
        return pl.ds((2**level - 1) * ROWS, 2**level * ROWS)

    diag_loads = [
        pltpu.make_async_copy(
            diag_hbm.at[rows_of(level), :],
            diag_ref.at[rows_of(level), :],
            load_sem.at[level],
        )
        for level in range(LEVELS)
    ]
    rhs_load = pltpu.make_async_copy(rhs_hbm, rhs_ref, load_sem.at[LEVELS])
    panels_load = pltpu.make_async_copy(panels_hbm, panels_ref, load_sem.at[LEVELS + 1])
    maps_load = pltpu.make_async_copy(maps_hbm, maps_ref, load_sem.at[LEVELS + 2])
    barrier = pltpu.get_barrier_semaphore()

    def greet(target):
        pl.semaphore_signal(
            barrier, inc=1, device_id=target, device_id_type=pl.DeviceIdType.MESH
        )

    for place in ring:
        greet(device(cube, peer(place)))
    for member in members(cube, n_cube):
        greet(device(member, blk))
    diag_loads[0].start()
    rhs_load.start()
    panels_load.start()
    maps_load.start()
    for load in diag_loads[1:]:
        load.start()

    def wide_of(level):
        return slice(3 * FOLD * (2**level - 1) * ROWS, 3 * FOLD * (2**(level + 1) - 1) * ROWS)

    def tall_of(level):
        return slice(FOLD * (2**level - 1) * ROWS, FOLD * (2**(level + 1) - 1) * ROWS)

    def folds_of(level):
        columns = diag_ref[rows_of(level), :].T
        span = columns.shape[1]
        parts = columns.reshape(n_blk, FOLD, SUB, span)
        return [parts[:, i].reshape(n_blk * SUB, span) for i in range(FOLD)]

    def beside(folds):
        return left_terms(jnp.concatenate(folds, axis=1))

    def below(folds):
        return left_terms(jnp.concatenate([fold.T for fold in folds], axis=0))

    def prepare_facts(level):
        reach = 2 * 2**level
        mine = lax.rem(cube, reach)
        row_ids = lax.broadcasted_iota(jnp.int32, (ROWS, MAPPED), 0)
        for half in range(2):
            onehot = (row_ids == maps_ref[level, half : half + 1, :]).astype(F32)
            mat = exact(onehot, panels_ref[level, half]) * (-1.0 / SCALE)
            facts[level, mine, half] = pack(mat)[0]
        for stream in range(STREAMS):
            rows = rhs_ref[level + 1, :, columns_of(stream)]
            facts[level, mine, 2 + stream] = pack(rows)[0]

    def exchange_facts(level):
        reach = 2 * 2**level
        base = cube - lax.rem(cube, reach)
        mine = lax.rem(cube, reach)
        for member in members(mine, reach):
            pltpu.make_async_remote_copy(
                src_ref=facts.at[level, mine],
                dst_ref=facts.at[level, mine],
                send_sem=fact_send_sem.at[level],
                recv_sem=fact_recv_sem.at[level],
                device_id=device(base + member, blk),
                device_id_type=pl.DeviceIdType.MESH,
            ).start()

    def combine(under):
        level = under + 1
        width = 2**under
        reach = 2 * width
        diag_loads[level].wait()
        wait_for(facts.at[under, pl.ds(0, reach - 1)], fact_recv_sem.at[under])
        zero = jnp.zeros((ROWS, ROWS), F32)
        lines = []
        for p in range(reach):
            line = [zero] * reach
            line[p] = unpack(facts[under, p, 0][None])
            line[p ^ width] = unpack(facts[under, p ^ width, 1][None])
            lines.append(jnp.concatenate(line, axis=1))
        update = jnp.concatenate(lines, axis=0)
        folds = folds_of(level)
        stacked = exact(jnp.concatenate(folds, axis=0), update)
        height = n_blk * SUB
        merged = [stacked[i * height : (i + 1) * height] for i in range(FOLD)]
        forward[:, wide_of(level)] = beside(merged)
        correct[tall_of(level), :] = below(merged)
        plain = beside(folds)
        for stream in range(STREAMS):
            rows = jnp.stack([facts[under, p, 2 + stream] for p in range(reach)])
            base_rows[stream, under] = dot(plain, spread_terms(rows))

    def prepare_backward(level):
        backward[tall_of(level), :] = below(folds_of(level))

    def wait_for(ref, sem):
        pltpu.make_async_copy(ref, ref, sem).wait()

    def scatter_start(stream, level, distances):
        def step(place):
            to = peer(place)
            pltpu.make_async_remote_copy(
                src_ref=part.at[stream, level, to],
                dst_ref=rs_recv.at[stream, level, blk],
                send_sem=rs_send_sem.at[stream, level],
                recv_sem=rs_recv_sem.at[stream, level],
                device_id=device(cube, to),
                device_id_type=pl.DeviceIdType.MESH,
            ).start()

        for place in ring:
            if place[0] in distances:
                step(place)

    def gather_start(stream, level):
        def step(place):
            to = peer(place)
            pltpu.make_async_remote_copy(
                src_ref=gather.at[stream, level, blk],
                dst_ref=gather.at[stream, level, blk],
                send_sem=ag_send_sem.at[stream, level],
                recv_sem=ag_recv_sem.at[stream, level],
                device_id=device(cube, to),
                device_id_type=pl.DeviceIdType.MESH,
            ).start()

        for place in ring:
            step(place)

    others = pl.ds(0, n_blk - 1)
    streams = range(STREAMS)

    def columns_of(stream):
        return pl.ds(stream * COLS, COLS)

    def scatter(stream, level, entry):
        terms = spread_terms(entry)
        slab = n_y * SUB
        for distances in halves:
            planes = [lax.rem(plane + dz, depth) for dz in distances]
            starts = [pl.multiple_of(at * slab, slab) for at in planes]
            rows = jnp.concatenate(
                [forward[pl.ds(at, slab), wide_of(level)] for at in starts], axis=0
            )
            products = dot(rows, terms)
            for i, at in enumerate(planes):
                piece = products[i * slab : (i + 1) * slab]
                if level:
                    known = base_rows[stream, level - 1, pl.ds(starts[i], slab)]
                    piece = known + SCALE * piece
                part[stream, level, pl.ds(at * n_y, n_y)] = piece.reshape(n_y, SUB, LANES)
            if level == 0 and stream == 0 and distances is halves[0]:
                pl.semaphore_wait(barrier, n_blk + n_cube - 2)
            scatter_start(stream, level, distances)
        rs_recv[stream, level, blk] = part[stream, level, blk]

    def climb(stream, level):
        wait_for(rs_recv.at[stream, level, others], rs_recv_sem.at[stream, level])
        rows = jnp.sum(rs_recv[stream, level], axis=0)
        if level + 1 == LEVELS:
            gather[stream, level, blk] = rows
            gather_start(stream, level)
            return
        reach = 2 * 2**level
        base = cube - lax.rem(cube, reach)
        mine = lax.rem(cube, reach)
        spread[stream, level, mine] = rows
        for member in members(mine, reach):
            pltpu.make_async_remote_copy(
                src_ref=spread.at[stream, level, mine],
                dst_ref=spread.at[stream, level, mine],
                send_sem=up_send_sem.at[stream, level],
                recv_sem=up_recv_sem.at[stream, level],
                device_id=device(base + member, blk),
                device_id_type=pl.DeviceIdType.MESH,
            ).start()
        solved[stream, level] = rows

    def enter(stream, level):
        if level + 1 == LEVELS:
            return
        reach = 2 * 2**level
        wait_for(
            spread.at[stream, level, pl.ds(0, reach - 1)], up_recv_sem.at[stream, level]
        )
        scatter(stream, level + 1, spread[stream, level, :reach])

    def send_down(stream, level, source, target, send_sem, recv_sem):
        width = 2**level
        under = level - 1
        base = cube - lax.rem(cube, width)
        mine = lax.rem(cube, width)
        for member in members(mine, width):
            pltpu.make_async_remote_copy(
                src_ref=source.at[stream, under, member],
                dst_ref=target.at[stream, under, mine],
                send_sem=send_sem.at[stream, under],
                recv_sem=recv_sem.at[stream, under],
                device_id=device(base + member, blk),
                device_id_type=pl.DeviceIdType.MESH,
            ).start()
        target[stream, under, mine] = source[stream, under, mine]

    def receive_down(stream, level, target, recv_sem):
        width = 2**level
        under = level - 1
        wait_for(
            target.at[stream, under, pl.ds(0, width - 1)], recv_sem.at[stream, under]
        )
        return jnp.sum(target[stream, under, :width], axis=0)

    def descend(stream, level):
        width = 2**level
        wait_for(gather.at[stream, level, others], ag_recv_sem.at[stream, level])
        work = right_terms(gather[stream, level].reshape(n_blk * SUB, LANES))
        if level:
            sums = collect_terms(dot(correct[tall_of(level), :], work), width)
            sums_send[stream, level - 1, :width] = sums
            send_down(stream, level, sums_send, sums_recv, down_send_sem, down_recv_sem)
        rows = collect_terms(dot(backward[tall_of(level), :], work), width)
        if level:
            rows_send[stream, level - 1, :width] = rows
            send_down(stream, level, rows_send, rows_recv, rows_send_sem, rows_recv_sem)
        else:
            out_ref[0, :, columns_of(stream)] = unpack(rows)

    def leave(stream, level):
        if level == 0:
            return
        under = level - 1
        sums = receive_down(stream, level, sums_recv, down_recv_sem)
        gather[stream, under, blk] = solved[stream, under] + SCALE * sums
        gather_start(stream, under)

    def finish(stream, level):
        if level:
            rows = receive_down(stream, level, rows_recv, rows_recv_sem)
            out_ref[level, :, columns_of(stream)] = unpack(rows[None])

    diag_loads[0].wait()
    forward[:, wide_of(0)] = beside(folds_of(0))
    rhs_load.wait()
    for stream in streams:
        scatter(stream, 0, pack(rhs_ref[0, :, columns_of(stream)]))
        if stream == 0:
            panels_load.wait()
            maps_load.wait()
            for level in range(LEVELS - 1):
                prepare_facts(level)
                exchange_facts(level)
    combine(0)

    def in_turn(first, second, level, interleave):
        if interleave:
            for stream in streams:
                first(stream, level)
            for stream in streams:
                second(stream, level)
        else:
            for stream in streams:
                first(stream, level)
                second(stream, level)

    def drain_up(level):
        for stream in streams:
            wait_for(part.at[stream, level, others], rs_send_sem.at[stream, level])
            if level + 1 < LEVELS:
                rest = pl.ds(0, 2 * 2**level - 1)
                wait_for(spread.at[stream, level, rest], up_send_sem.at[stream, level])
        if level + 1 < LEVELS:
            wait_for(facts.at[level, rest], fact_send_sem.at[level])

    def drain_down(level):
        rest = pl.ds(0, 2**level - 1)
        for stream in streams:
            wait_for(gather.at[stream, level, others], ag_send_sem.at[stream, level])
            for source, sem in ((sums_send, down_send_sem), (rows_send, rows_send_sem)):
                wait_for(source.at[stream, level - 1, rest], sem.at[stream, level - 1])

    for level in range(LEVELS):
        in_turn(climb, enter, level, UP_TURNS[level])
        drain_up(level)
        if level + 2 < LEVELS:
            combine(level + 1)
        elif level + 2 == LEVELS:
            prepare_backward(LEVELS - 1)
            prepare_backward(LEVELS - 2)
        else:
            for low in range(LEVELS - 2):
                prepare_backward(low)
    for level in reversed(range(LEVELS)):
        in_turn(descend, leave, level, DOWN_TURNS[level])
        if level:
            for stream in streams:
                finish(stream, level)
            drain_down(level)

    for stream in streams:
        wait_for(gather.at[stream, 0, others], ag_send_sem.at[stream, 0])


def body(n_cube, n_blk, right_side, diag_inverse, panels, extend_map):
    rhs = right_side[:, 0, 0]
    blocks = panels[:, 0, 0]
    maps = extend_map[:, 0, 0]
    rows, columns = diag_inverse.shape
    widest = 2 ** (LEVELS - 1)
    vmem = pl.BlockSpec(memory_space=pltpu.VMEM)
    chunks = pltpu.VMEM((STREAMS, LEVELS, n_blk, SUB, LANES), F32)
    sets = pltpu.VMEM((STREAMS, LEVELS - 1, widest, SUB, LANES), F32)
    result = pl.pallas_call(
        functools.partial(kernel, n_cube, n_blk),
        out_shape=jax.ShapeDtypeStruct(rhs.shape, F32),
        in_specs=[pl.BlockSpec(memory_space=pltpu.HBM)] * 4,
        out_specs=vmem,
        scratch_shapes=[
            pltpu.VMEM(rhs.shape, F32),
            pltpu.VMEM(diag_inverse.shape, F32),
            pltpu.VMEM(blocks.shape, F32),
            pltpu.VMEM(maps.shape, jnp.int32),
            pltpu.VMEM((n_blk * SUB, 3 * FOLD * rows), BF16),
            pltpu.VMEM((FOLD * rows, 3 * n_blk * SUB), BF16),
            pltpu.VMEM((FOLD * rows, 3 * n_blk * SUB), BF16),
            pltpu.VMEM((STREAMS, LEVELS - 1, n_blk * SUB, LANES), F32),
            pltpu.VMEM((LEVELS - 1, widest, 2 + STREAMS, SUB, LANES), F32),
            pltpu.VMEM((STREAMS, LEVELS - 1, SUB, LANES), F32),
            chunks,
            chunks,
            chunks,
            sets,
            sets,
            sets,
            sets,
            sets,
        ]
        + [pltpu.SemaphoreType.DMA((STREAMS, LEVELS))] * 4
        + [pltpu.SemaphoreType.DMA((STREAMS, LEVELS - 1))] * 6
        + [pltpu.SemaphoreType.DMA((LEVELS - 1,))] * 2
        + [pltpu.SemaphoreType.DMA((LEVELS + 3,))],
        compiler_params=pltpu.CompilerParams(
            collective_id=0, has_side_effects=True, vmem_limit_bytes=40 * 2**20
        ),
    )(*[pltpu.with_memory_space_constraint(x, pltpu.HBM) for x in (rhs, diag_inverse, blocks, maps)])
    return result[:, None, None]


def solution(mesh):
    placed = (
        P(None, "cube", "blk", None, None),
        P("cube", "blk"),
        P(None, "cube", "blk", None, None, None),
        P(None, "cube", "blk", None, None),
    )
    return jax.shard_map(
        functools.partial(body, mesh.shape["cube"], mesh.shape["blk"]),
        mesh=mesh,
        in_specs=placed,
        out_specs=P(None, "cube", "blk", None, None),
        check_vma=False,
    )
```
